512 devices in a mesh: dp: 64 (over x, z), tensor: 8 (over y, core).
Axes of the slice: x: 4, y: 4, z: 16, core: 2. Of those that a mesh axis runs over, the one named last changes fastest.
Arguments:
- residual: bfloat16 [2048, 6144], P('dp', 'tensor'), may hold values from -16 to 16
- queries: bfloat16 [2048, 6144], P('dp', 'tensor'), may hold values from -4.5 to 4.5
- keys: bfloat16 [2048, 128, 1024], P('dp', None, 'tensor'), may hold values from -4.5 to 4.5
- values: bfloat16 [2048, 128, 1024], P('dp', None, 'tensor'), may hold values from -6 to 6
- lengths: int32 [2048], P('dp'), may hold values from 2 to 128
- norm_gain: bfloat16 [6144], P('tensor'), may hold values from 0.099609375 to 1.8984375
- expert_ids: int32 [2048, 2], P('dp'), may hold values from 0 to 7, all different within a row; in each aligned block of 32 rows (0 to 31, 32 to 63, ...) at most 16 rows name the same one
- expert_weights: float32 [2048, 2], P('dp'), may hold values from 0.2 to 1
- w_in: bfloat16 [6144, 65536], P('tensor', 'dp'), may hold values from -0.078125 to 0.078125
- w_out: bfloat16 [65536, 6144], P('dp', 'tensor'), may hold values from -0.0625 to 0.0625
Outputs:
- output: bfloat16 [2048, 6144], P('dp', 'tensor')
The draws below stay inside these ranges and needn't reach their ends.
Inputs may be any that keep to these rules, and one draw needn't show every extreme that they name: `expert_ids`: each token names 2 different experts; at most 16 of the tokens of one index of dp name one expert, and in every draw some expert is named by exactly 16 of them.
All inputs are finite; a program needn't handle non-finite values.
Results may differ from the reference program's by a relative error of at most 0.008.
Values may be sent and summed in bfloat16 or wider, within the bound.
No kernel may reach another device: no remote copies, remote signals or barrier semaphores. Data moves between devices by JAX's collectives and lax.ppermute only.
A program may use at most 64 MiB of HBM per device.

```python
import math
import jax
import jax.numpy as jnp
import numpy as np
from jax import lax

D = 6144
HEADS = 48
KV = 8
HEAD = 128
EXPERTS = 8
TOPK = 2
FF = 8192
CACHE = 128
TOK_DEV = 32
SRC_CAP = 16
TOKENS = 2048
CAP = 384


def draw_residual(key, part):
    key_base, key_rough = jax.random.split(jax.random.fold_in(key, 101), 2)
    base = jax.random.normal(key_base, (TOKENS, D), jnp.float32)
    rough = jax.random.uniform(key_rough, (D,), jnp.float32, 0.5, 1.5)
    column = jnp.arange(D, dtype=jnp.float32) / (D - 1)
    rising = jnp.exp(math.log(3.0) * column) * 0.6
    drawn = base * rising[None, :] * rough[None, :]
    return jnp.clip(drawn, -16.0, 16.0).astype(jnp.bfloat16)


def attention_draw(key):
    key_query, key_cached = jax.random.split(jax.random.fold_in(key, 202), 2)
    queries = jnp.clip(jax.random.normal(key_query, (TOKENS, HEADS * HEAD), jnp.float32), -4.5, 4.5)
    cached = jnp.clip(jax.random.normal(key_cached, (TOKENS, CACHE, KV * HEAD), jnp.float32), -4.5, 4.5)
    return (queries.astype(jnp.bfloat16), cached.astype(jnp.bfloat16))


def draw_queries(key, part):
    return attention_draw(key)[0]


def draw_keys(key, part):
    return attention_draw(key)[1]


def touch_ends(values, key, smallest, top_value):
    longest = values.shape.index(max(values.shape))
    spots = []
    for shift in (0, 1):
        where = [jax.random.randint(jax.random.fold_in(key, axis), (), 0, length) for axis, length in enumerate(values.shape)]
        where[longest] = (where[longest] + shift) % values.shape[longest]
        spots.append(tuple(where))
    return values.at[spots[0]].set(smallest).at[spots[1]].set(top_value)


def steps_of(stream_key, dims, pieces, smallest, high):
    level, own = 1.0, jax.random.fold_in(stream_key, 6)
    for position, parts in pieces:
        draws = jnp.exp(jax.random.uniform(jax.random.fold_in(own, position), (parts,), jnp.float32, smallest / len(pieces), high / len(pieces)))
        level = level * jnp.repeat(draws, dims[position] // parts).reshape([-1 if axis == position else 1 for axis in range(len(dims))])
    return level


def assign_block(stream_key, own, number, rows, number_of, top, limit, lean):
    ranking = jax.random.permutation(stream_key, number_of)
    packed, usual = portions_of(number_of, rows * top, limit, lean, True), portions_of(number_of, rows * top, limit, lean, False)
    places = jnp.arange(number_of)

    def named(sizes, rotation):
        used = int((sizes > 0).sum())
        fixed = max(1, used // 4)
        passed = fixed + (places - fixed + rotation * (used - fixed)) % max(1, number_of - fixed)
        return jnp.zeros((number_of,), jnp.int32).at[ranking[jnp.where(places < fixed, places, passed)]].set(jnp.asarray(sizes, jnp.int32))

    sizes = jnp.where(number % 4 == 0, named(packed, number // 4), named(usual, number - number // 4 - 1))
    mixed = jax.random.permutation(jax.random.fold_in(own, 3), number_of)
    donor, sink = mixed[0:number_of // 2 * 2:2], mixed[1:number_of // 2 * 2:2]
    margin = jnp.minimum(sizes[donor] - 1, limit - sizes[sink]) // 2
    margin = jnp.where((donor == ranking[0]) | (sink == ranking[0]) | (sizes[sink] == 0), 0, jnp.maximum(margin, 0))
    passed = jax.random.randint(jax.random.fold_in(own, 4), (number_of // 2,), 0, 1 << 20) % (margin + 1)
    sizes = sizes.at[donor].add(-passed).at[sink].add(passed)
    items = jnp.searchsorted(jnp.cumsum(sizes), jnp.arange(rows * top), side="right").astype(jnp.int32)
    table = items.reshape(top, rows).T
    table = table[jax.random.permutation(jax.random.fold_in(own, 1), rows)]
    rotation = jax.random.randint(jax.random.fold_in(own, 2), (rows, 1), 0, top)
    return jnp.take_along_axis(table, (jnp.arange(top)[None, :] + rotation) % top, axis=1)


def portions_of(amount, total, reach, lean, full):
    portions = [(1 << 20) // math.isqrt(standing ** lean) + 1 for standing in range(1, amount + 1)]
    largest = reach if full else min(reach, max(-(-total // amount), total * portions[0] // sum(portions)))
    least = 1 if total - largest >= amount - 1 else 0
    holding, rest = [largest] + [least] * (amount - 1), total - largest - least * (amount - 1)
    while rest > 0:
        movable = [i for i in range(1, amount) if holding[i] < largest] or [i for i in range(1, amount) if holding[i] < reach]
        mass, budget = sum([portions[i] for i in movable]), rest
        for i in movable:
            more = min(reach - holding[i], max(1, budget * portions[i] // mass), rest)
            holding[i] = holding[i] + more
            rest = rest - more
    return np.array(holding)


def normal_values(key, shape, width, most, cuts=(), kind=jnp.bfloat16):
    values = width * jax.random.normal(key, shape, jnp.float32)
    if cuts:
        values = values * steps_of(key, shape, cuts, -0.22, 0.18)
    return jnp.clip(values, -most, most).astype(kind)


def setup_inputs(seed: int = 0) -> dict:
    streams_of = jax.random.split(jax.random.key(seed), 11)
    residual = draw_residual(jax.random.fold_in(streams_of[10], 71), 0)
    queries = draw_queries(jax.random.fold_in(streams_of[10], 71), 0)
    keys = draw_keys(jax.random.fold_in(streams_of[10], 71), 0)
    values = normal_values(streams_of[3], (TOKENS, CACHE, KV * HEAD), 1.0, 6.0, ((0, 64), (2, 8)))
    lengths = touch_ends(jax.random.randint(streams_of[4], (TOKENS,), 2, CACHE + 1), jax.random.fold_in(streams_of[4], 1), 2, CACHE).astype(jnp.int32)
    norm_gain = jnp.clip(1.0 + 0.18 * jax.random.normal(streams_of[5], (D,), jnp.float32), 0.099609375, 1.8984375).astype(jnp.bfloat16)
    expert_ids_keys = jax.random.split(jax.random.fold_in(streams_of[6], 1), TOKENS // TOK_DEV)
    expert_ids_turns = jax.random.permutation(jax.random.fold_in(streams_of[6], 3), TOKENS // TOK_DEV)
    expert_ids = jax.vmap(lambda own, number: assign_block(jax.random.fold_in(streams_of[6], 2), own, number, TOK_DEV, EXPERTS, TOPK, SRC_CAP, 2))(expert_ids_keys, expert_ids_turns).reshape((TOKENS, TOPK))
    expert_weights = jnp.clip(0.2 + 0.8 * jax.random.uniform(streams_of[7], (TOKENS, TOPK), jnp.float32) ** steps_of(streams_of[7], (TOKENS, TOPK), ((0, 64),), -0.2, 0.2), 0.2, 1.0)
    w_in = normal_values(streams_of[8], (D, EXPERTS * FF), D ** -0.5, 0.078125, ((0, 8), (1, 64)))
    w_out = normal_values(streams_of[9], (EXPERTS * FF, D), FF ** -0.5, 0.0625, ((0, 64), (1, 8)))
    return {"residual": residual, "queries": queries, "keys": keys, "values": values, "lengths": lengths, "norm_gain": norm_gain, "expert_ids": expert_ids, "expert_weights": expert_weights, "w_in": w_in, "w_out": w_out}


NORM_EPSILON = 1e-05

def attention_rows(residual, queries, keys, values, lengths):
    group_size = HEADS // KV
    query_float = queries.astype(jnp.float32).reshape(TOKENS, KV, group_size, HEAD)
    key_float = keys.astype(jnp.float32).reshape(TOKENS, CACHE, KV, HEAD)
    value_float = values.astype(jnp.float32).reshape(TOKENS, CACHE, KV, HEAD)
    scores = jnp.einsum('tgjd,tlgd->tgjl', query_float, key_float) * HEAD ** (-0.5)
    live_mask = (jnp.arange(CACHE, dtype=jnp.int32)[None, :] < lengths[:, None])[:, None, None, :]
    scores = jnp.where(live_mask, scores, -1e+30)
    peak_score = lax.optimization_barrier(jnp.max(scores, axis=-1, keepdims=True))
    powered = jnp.exp(scores - peak_score)
    attention_probs = (powered / lax.optimization_barrier(jnp.sum(powered, axis=-1, keepdims=True))).astype(jnp.bfloat16)
    attended = jnp.einsum('tgjl,tlgd->tgjd', attention_probs.astype(jnp.float32), value_float)
    return residual.astype(jnp.float32) + attended.reshape(TOKENS, D)

def reference(residual, queries, keys, values, lengths, norm_gain, expert_ids, expert_weights, w_in, w_out):
    summed = attention_rows(residual, queries, keys, values, lengths)
    square_sums = lax.optimization_barrier(jnp.sum(summed * summed, axis=1, keepdims=True))
    normed = (summed * lax.rsqrt(square_sums / D + NORM_EPSILON) * norm_gain.astype(jnp.float32)).astype(jnp.bfloat16)
    flat_ids = expert_ids.reshape(-1)
    pair_count = TOKENS * TOPK
    onehot = (flat_ids[:, None] == jnp.arange(EXPERTS, dtype=jnp.int32)[None, :]).astype(jnp.int32)
    earlier = jnp.cumsum(onehot, axis=0, dtype=jnp.int32) - onehot
    slot_index = lax.optimization_barrier(jnp.sum(earlier * onehot, axis=1, dtype=jnp.int32))
    capacity = CAP
    keep_mask = slot_index < capacity
    token_index = jnp.arange(pair_count, dtype=jnp.int32) // TOPK
    padded_rows = jnp.concatenate([normed, jnp.zeros((1, D), jnp.bfloat16)], axis=0)
    pair_out = jnp.zeros((pair_count, D), jnp.float32)
    for expert in range(EXPERTS):
        chosen = (flat_ids == expert) & keep_mask
        target = jnp.where(chosen, slot_index, capacity).astype(jnp.int32)
        source_row = jnp.full((capacity,), TOKENS, jnp.int32).at[target].set(token_index, mode='drop')
        gathered = padded_rows[source_row]
        hidden = jax.nn.silu(jnp.dot(gathered, w_in[:, expert * FF:(expert + 1) * FF], preferred_element_type=jnp.float32)).astype(jnp.bfloat16)
        produced = jnp.dot(hidden, w_out[expert * FF:(expert + 1) * FF], preferred_element_type=jnp.float32)
        padded_out = jnp.concatenate([produced, jnp.zeros((1, D), jnp.float32)], axis=0)
        pair_out = pair_out + padded_out[target]
    weighted = pair_out * expert_weights.reshape(-1)[:, None]
    output = summed + lax.optimization_barrier(jnp.sum(weighted.reshape(TOKENS, TOPK, D), axis=1))
    return output.astype(jnp.bfloat16)
```

```python
import jax
import jax.numpy as jnp
from jax import lax
from jax.sharding import Mesh, PartitionSpec as P

HEADS = 48
KV = 8
HEAD = 128
D = 6144
EXPERTS = 8
TOPK = 2
CACHE = 128
SRC_CAP = 16
BLOCKS = 64
CLASSES = 4
PER_CLASS = SRC_CAP // CLASSES
CAPACITY = 384
CLASS_ROWS = CAPACITY // CLASSES + BLOCKS * 6 // (4 * CLASSES)
META = 128

NORM_EPSILON = 1e-05

DP = ("x", "zh", "zq", "zn")
TENSOR = ("y", "core")


def attend(residual, queries, keys, values, lengths):
    tokens, width = residual.shape
    group_size = HEADS // KV
    query_rows = queries.reshape(tokens, group_size, HEAD)
    scores = jnp.einsum(
        "tjd,tld->tjl", query_rows, keys, preferred_element_type=jnp.float32
    ) * HEAD ** (-0.5)
    live_mask = (jnp.arange(CACHE, dtype=jnp.int32)[None, :] < lengths[:, None])[:, None, :]
    scores = jnp.where(live_mask, scores, -1e30)
    peak_score = jnp.max(scores, axis=-1, keepdims=True)
    powered = jnp.exp(scores - peak_score)
    probs = (powered / jnp.sum(powered, axis=-1, keepdims=True)).astype(jnp.bfloat16)
    attended = jnp.einsum("tjl,tld->tjd", probs, values, preferred_element_type=jnp.float32)
    return residual.astype(jnp.float32) + attended.reshape(tokens, width)


def copies_to(value, axis, peers):
    copies = jnp.broadcast_to(value, (peers, *value.shape))
    return lax.all_to_all(copies, axis, split_axis=0, concat_axis=0, tiled=True)


def summed_at_owner(pieces, axis):
    return jnp.sum(
        lax.all_to_all(pieces, axis, split_axis=0, concat_axis=0, tiled=True).astype(jnp.float32), axis=0
    )


def earlier_sum(counts):
    before = jnp.arange(BLOCKS)[:, None] > jnp.arange(BLOCKS)[None, :]
    return jnp.sum(jnp.where(before, counts[None, :], 0), axis=1)


def shards(
    residual, queries, keys, values, lengths, norm_gain, expert_ids, expert_weights, w_in, w_out
):
    tokens, width = residual.shape
    block = ((lax.axis_index("x") * 2 + lax.axis_index("zh")) * 2 + lax.axis_index("zq")) * 4 + lax.axis_index("zn")
    own_class = lax.axis_index("zn")

    summed = attend(residual, queries, keys, values, lengths)
    square_sums = lax.psum(jnp.sum(summed * summed, axis=1), TENSOR)
    normed = (
        summed
        * lax.rsqrt(square_sums[:, None] / D + NORM_EPSILON)
        * norm_gain.astype(jnp.float32)[None, :]
    ).astype(jnp.bfloat16)

    flat_ids = expert_ids.reshape(-1)
    pairs = flat_ids.shape[0]
    same = flat_ids[:, None] == flat_ids[None, :]
    earlier = jnp.arange(pairs)[:, None] > jnp.arange(pairs)[None, :]
    rank = jnp.sum((same & earlier).astype(jnp.int32), axis=1)
    slots = EXPERTS * SRC_CAP
    target = flat_ids * SRC_CAP + (rank + block) % CLASSES * PER_CLASS + rank // CLASSES
    pick_pairs = target[None, :] == jnp.arange(slots, dtype=jnp.int32)[:, None]
    pick_tokens = jnp.sum(
        pick_pairs.reshape(slots, tokens, TOPK).astype(jnp.float32), axis=2
    ).astype(jnp.bfloat16)
    counts = jnp.sum(
        (flat_ids[None, :] == jnp.arange(EXPERTS, dtype=jnp.int32)[:, None]).astype(jnp.float32), axis=1
    ).astype(jnp.bfloat16)

    packed = jnp.dot(pick_tokens, normed, preferred_element_type=jnp.float32).astype(jnp.bfloat16)
    packed = packed.reshape(EXPERTS, 1, CLASSES, PER_CLASS, width)
    meta = jnp.broadcast_to(counts[:, None, None, None, None], (EXPERTS, 1, CLASSES, PER_CLASS, META))
    outgoing = jnp.concatenate([packed, meta], axis=-1)
    outgoing = jnp.broadcast_to(outgoing, (EXPERTS, 2, CLASSES, PER_CLASS, width + META))
    received = lax.all_to_all(
        outgoing.reshape(BLOCKS, PER_CLASS, width + META), DP, split_axis=0, concat_axis=0, tiled=True
    )

    named = received[:, 0, width].astype(jnp.int32)
    kept = jnp.clip(CAPACITY - earlier_sum(named), 0, named)
    shift = (own_class - jnp.arange(BLOCKS, dtype=jnp.int32)) % CLASSES
    in_class = (kept - shift + CLASSES - 1) // CLASSES
    first = earlier_sum(in_class)
    place = jnp.arange(PER_CLASS, dtype=jnp.int32)[None, :]
    spot = jnp.where(place < in_class[:, None], first[:, None] + place, -1).reshape(-1)
    compact = (spot[None, :] == jnp.arange(CLASS_ROWS, dtype=jnp.int32)[:, None]).astype(jnp.bfloat16)
    class_rows = jnp.dot(
        compact,
        received[:, :, :width].reshape(BLOCKS * PER_CLASS, width),
        preferred_element_type=jnp.float32,
    ).astype(jnp.bfloat16)

    rows = copies_to(class_rows, "zn", CLASSES).reshape(CLASSES * CLASS_ROWS, width)
    total = rows.shape[0]
    hidden_parts = jnp.dot(rows, w_in, preferred_element_type=jnp.float32).astype(jnp.bfloat16)
    unit = hidden_parts.shape[1] // 8
    pieces = jnp.moveaxis(hidden_parts.reshape(total, 2, 4, unit), 0, 2)
    core_sums = summed_at_owner(pieces, "core").astype(jnp.bfloat16)
    hidden = jax.nn.silu(summed_at_owner(core_sums.reshape(4, total, unit), "y")).astype(jnp.bfloat16)
    gathered = copies_to(hidden, "y", 4)
    gathered = lax.all_gather(gathered, "core", axis=0, tiled=True)
    hidden_all = jnp.moveaxis(gathered, 0, 1).reshape(total, 8 * unit)
    results = jnp.dot(hidden_all, w_out, preferred_element_type=jnp.float32).astype(jnp.bfloat16)

    class_out = summed_at_owner(results.reshape(CLASSES, CLASS_ROWS, width), "zn").astype(jnp.bfloat16)
    spread = (spot[:, None] == jnp.arange(CLASS_ROWS, dtype=jnp.int32)[None, :]).astype(jnp.bfloat16)
    returned = jnp.dot(spread, class_out, preferred_element_type=jnp.float32).astype(jnp.bfloat16)
    combined = lax.all_to_all(
        returned.reshape(BLOCKS, PER_CLASS, width), DP, split_axis=0, concat_axis=0, tiled=True
    )
    per_expert = jnp.sum(
        combined.reshape(EXPERTS, 2, SRC_CAP, width).astype(jnp.float32), axis=1
    ).reshape(slots, width)
    mix_rows = jnp.sum(
        (pick_pairs.astype(jnp.float32) * expert_weights.reshape(-1)[None, :]).reshape(slots, tokens, TOPK),
        axis=2,
    )
    addition = jnp.einsum("st,sd->td", mix_rows, per_expert, precision=lax.Precision.HIGHEST)
    return (summed + addition).astype(jnp.bfloat16)


def solution(mesh):
    fine = Mesh(mesh.devices.reshape(4, 2, 2, 4, 4, 2), (*DP, *TENSOR))
    in_specs = (
        P(DP, TENSOR),
        P(DP, TENSOR),
        P(DP, None, TENSOR),
        P(DP, None, TENSOR),
        P(DP),
        P(TENSOR),
        P(DP, None),
        P(DP, None),
        P(TENSOR, DP),
        P(DP, TENSOR),
    )
    return jax.shard_map(shards, mesh=fine, in_specs=in_specs, out_specs=P(DP, TENSOR), check_vma=False)
```

```python
import jax
import jax.numpy as jnp
from jax import lax
from jax.experimental import pallas as pl
from jax.experimental.pallas import tpu as pltpu
from jax.sharding import Mesh, PartitionSpec as P

HEADS = 48
KV = 8
HEAD = 128
D = 6144
EXPERTS = 8
TOPK = 2
CACHE = 128
SRC_CAP = 16
BLOCKS = 64
CLASSES = 4
PER_CLASS = SRC_CAP // CLASSES
CAPACITY = 384
CLASS_ROWS = CAPACITY // CLASSES + BLOCKS * 6 // (4 * CLASSES)
META = 128
ROWS = CLASSES * CLASS_ROWS
SQUARES = 16
UNIT = 128

NORM_EPSILON = 1e-05

DP = ("x", "zh", "zq", "zn")
TENSOR = ("y", "core")


def attend(residual, queries, keys, values, lengths):
    tokens, width = residual.shape
    group_size = HEADS // KV
    query_rows = queries.reshape(tokens, group_size, HEAD)
    scores = jnp.einsum(
        "tjd,tld->tjl", query_rows, keys, preferred_element_type=jnp.float32
    ) * HEAD ** (-0.5)
    live_mask = (jnp.arange(CACHE, dtype=jnp.int32)[None, :] < lengths[:, None])[:, None, :]
    scores = jnp.where(live_mask, scores, -1e30)
    peak_score = jnp.max(scores, axis=-1, keepdims=True)
    powered = jnp.exp(scores - peak_score)
    probs = (powered / jnp.sum(powered, axis=-1, keepdims=True)).astype(jnp.bfloat16)
    attended = jnp.einsum("tjl,tld->tjd", probs, values, preferred_element_type=jnp.float32)
    return residual.astype(jnp.float32) + attended.reshape(tokens, width)


def copies_to(value, axis, peers):
    copies = jnp.broadcast_to(value, (peers, *value.shape))
    return lax.all_to_all(copies, axis, split_axis=0, concat_axis=0, tiled=True)


def summed_at_owner(pieces, axis):
    return jnp.sum(
        lax.all_to_all(pieces, axis, split_axis=0, concat_axis=0, tiled=True).astype(jnp.float32), axis=0
    )


def diagonal():
    row = lax.broadcasted_iota(jnp.int32, (CLASS_ROWS, UNIT), 0)
    return row == lax.broadcasted_iota(jnp.int32, (CLASS_ROWS, UNIT), 1)


def leading_and_rest(sums):
    leading = sums.astype(jnp.bfloat16)
    return jnp.concatenate([leading, (sums - leading.astype(jnp.float32)).astype(jnp.bfloat16)], axis=0)


def hidden_kernel(rows_ref, gain_ref, w_ref, out_ref, scaled_ref, squares_ref):
    @pl.when(pl.program_id(0) == 0)
    def _():
        wide = rows_ref[...].astype(jnp.float32)
        scaled_ref[...] = (wide * gain_ref[...].astype(jnp.float32)).astype(jnp.bfloat16)
        sums = jnp.sum(wide * wide, axis=1, keepdims=True)
        lines = [
            jnp.sum(
                jnp.where(diagonal(), sums[c * CLASS_ROWS : (c + 1) * CLASS_ROWS], 0.0),
                axis=0,
                keepdims=True,
            )
            for c in range(CLASSES)
        ]
        lines.append(jnp.zeros((SQUARES // 2 - CLASSES, UNIT), jnp.float32))
        squares_ref[...] = leading_and_rest(jnp.concatenate(lines, axis=0))

    sums = jnp.dot(scaled_ref[...], w_ref[...], preferred_element_type=jnp.float32)
    for half in range(2):
        out_ref[half, :ROWS] = sums[:, half * UNIT : (half + 1) * UNIT].astype(jnp.bfloat16)
        out_ref[half, ROWS:] = squares_ref[...]


def hidden_pieces(rows, norm_gain, w_in):
    width, units = w_in.shape
    return pl.pallas_call(
        hidden_kernel,
        grid=(units // (2 * UNIT),),
        in_specs=[
            pl.BlockSpec((ROWS, width), lambda i: (0, 0)),
            pl.BlockSpec((1, width), lambda i: (0, 0)),
            pl.BlockSpec((width, 2 * UNIT), lambda i: (0, i)),
        ],
        out_specs=pl.BlockSpec((2, ROWS + SQUARES, UNIT), lambda i: (i, 0, 0)),
        out_shape=jax.ShapeDtypeStruct((units // UNIT, ROWS + SQUARES, UNIT), jnp.bfloat16),
        scratch_shapes=[
            pltpu.VMEM((ROWS, width), jnp.bfloat16),
            pltpu.VMEM((SQUARES, UNIT), jnp.bfloat16),
        ],
        compiler_params=pltpu.CompilerParams(vmem_limit_bytes=32 << 20),
        name="hidden_pieces",
    )(rows, norm_gain.reshape(1, width), w_in)


def core_kernel(in_ref, out_ref):
    out_ref[:, :ROWS] = (
        in_ref[0, :, :ROWS].astype(jnp.float32) + in_ref[1, :, :ROWS].astype(jnp.float32)
    ).astype(jnp.bfloat16)
    both = in_ref[0, 0, ROWS:].astype(jnp.float32) + in_ref[1, 0, ROWS:].astype(jnp.float32)
    split = leading_and_rest(both[: SQUARES // 2] + both[SQUARES // 2 :])
    for piece in range(out_ref.shape[0]):
        out_ref[piece, ROWS:] = split


def core_summed(pieces):
    return pl.pallas_call(
        core_kernel,
        out_shape=jax.ShapeDtypeStruct(pieces.shape[1:], jnp.bfloat16),
        compiler_params=pltpu.CompilerParams(vmem_limit_bytes=32 << 20),
        name="core_summed",
    )(pieces)


def silu_kernel(in_ref, out_ref):
    total = in_ref[0].astype(jnp.float32)
    for piece in range(1, in_ref.shape[0]):
        total = total + in_ref[piece].astype(jnp.float32)
    squares = total[ROWS : ROWS + SQUARES // 2] + total[ROWS + SQUARES // 2 :]
    for c in range(CLASSES):
        own = jnp.sum(jnp.where(diagonal(), squares[c : c + 1], 0.0), axis=1, keepdims=True)
        scaled = total[c * CLASS_ROWS : (c + 1) * CLASS_ROWS] * lax.rsqrt(own / D + NORM_EPSILON)
        hidden = (scaled / (1.0 + jnp.exp(-scaled))).astype(jnp.bfloat16)
        for piece in range(out_ref.shape[0]):
            out_ref[piece, c * CLASS_ROWS : (c + 1) * CLASS_ROWS] = hidden


def silu_copies(pieces):
    return pl.pallas_call(
        silu_kernel,
        out_shape=jax.ShapeDtypeStruct((pieces.shape[0], ROWS, UNIT), jnp.bfloat16),
        compiler_params=pltpu.CompilerParams(vmem_limit_bytes=32 << 20),
        name="silu_copies",
    )(pieces)


def earlier_sum(counts):
    before = jnp.arange(BLOCKS)[:, None] > jnp.arange(BLOCKS)[None, :]
    return jnp.sum(jnp.where(before, counts[None, :], 0), axis=1)


def shards(
    residual, queries, keys, values, lengths, norm_gain, expert_ids, expert_weights, w_in, w_out
):
    tokens, width = residual.shape
    block = ((lax.axis_index("x") * 2 + lax.axis_index("zh")) * 2 + lax.axis_index("zq")) * 4 + lax.axis_index("zn")
    own_class = lax.axis_index("zn")

    summed = attend(residual, queries, keys, values, lengths)
    unscaled = summed.astype(jnp.bfloat16)

    flat_ids = expert_ids.reshape(-1)
    pairs = flat_ids.shape[0]
    same = flat_ids[:, None] == flat_ids[None, :]
    earlier = jnp.arange(pairs)[:, None] > jnp.arange(pairs)[None, :]
    rank = jnp.sum((same & earlier).astype(jnp.int32), axis=1)
    slots = EXPERTS * SRC_CAP
    target = flat_ids * SRC_CAP + (rank + block) % CLASSES * PER_CLASS + rank // CLASSES
    pick_pairs = target[None, :] == jnp.arange(slots, dtype=jnp.int32)[:, None]
    pick_tokens = jnp.sum(
        pick_pairs.reshape(slots, tokens, TOPK).astype(jnp.float32), axis=2
    ).astype(jnp.bfloat16)
    counts = jnp.sum(
        (flat_ids[None, :] == jnp.arange(EXPERTS, dtype=jnp.int32)[:, None]).astype(jnp.float32), axis=1
    ).astype(jnp.bfloat16)

    packed = jnp.dot(pick_tokens, unscaled, preferred_element_type=jnp.float32).astype(jnp.bfloat16)
    packed = packed.reshape(EXPERTS, 1, CLASSES, PER_CLASS, width)
    meta = jnp.broadcast_to(counts[:, None, None, None, None], (EXPERTS, 1, CLASSES, PER_CLASS, META))
    outgoing = jnp.concatenate([packed, meta], axis=-1)
    outgoing = jnp.broadcast_to(outgoing, (EXPERTS, 2, CLASSES, PER_CLASS, width + META))
    received = lax.all_to_all(
        outgoing.reshape(BLOCKS, PER_CLASS, width + META), DP, split_axis=0, concat_axis=0, tiled=True
    )

    named = received[:, 0, width].astype(jnp.int32)
    kept = jnp.clip(CAPACITY - earlier_sum(named), 0, named)
    shift = (own_class - jnp.arange(BLOCKS, dtype=jnp.int32)) % CLASSES
    in_class = (kept - shift + CLASSES - 1) // CLASSES
    first = earlier_sum(in_class)
    place = jnp.arange(PER_CLASS, dtype=jnp.int32)[None, :]
    spot = jnp.where(place < in_class[:, None], first[:, None] + place, -1).reshape(-1)
    compact = (spot[None, :] == jnp.arange(CLASS_ROWS, dtype=jnp.int32)[:, None]).astype(jnp.bfloat16)
    class_rows = jnp.dot(
        compact,
        received[:, :, :width].reshape(BLOCKS * PER_CLASS, width),
        preferred_element_type=jnp.float32,
    ).astype(jnp.bfloat16)

    rows = copies_to(class_rows, "zn", CLASSES).reshape(ROWS, width)
    pieces = hidden_pieces(rows, norm_gain, w_in)
    pieces = lax.all_to_all(
        pieces.reshape(2, 4, ROWS + SQUARES, UNIT), "core", split_axis=0, concat_axis=0, tiled=True
    )
    pieces = lax.all_to_all(core_summed(pieces), "y", split_axis=0, concat_axis=0, tiled=True)
    gathered = lax.all_to_all(silu_copies(pieces), "y", split_axis=0, concat_axis=0, tiled=True)
    gathered = lax.all_gather(gathered, "core", axis=0, tiled=True)
    hidden = jnp.moveaxis(gathered, 0, 1).reshape(ROWS, 8 * UNIT)
    results = jnp.dot(hidden, w_out, preferred_element_type=jnp.float32).astype(jnp.bfloat16)

    class_out = summed_at_owner(results.reshape(CLASSES, CLASS_ROWS, width), "zn").astype(jnp.bfloat16)
    spread = (spot[:, None] == jnp.arange(CLASS_ROWS, dtype=jnp.int32)[None, :]).astype(jnp.bfloat16)
    returned = jnp.dot(spread, class_out, preferred_element_type=jnp.float32).astype(jnp.bfloat16)
    combined = lax.all_to_all(
        returned.reshape(BLOCKS, PER_CLASS, width), DP, split_axis=0, concat_axis=0, tiled=True
    )
    per_expert = jnp.sum(
        combined.reshape(EXPERTS, 2, SRC_CAP, width).astype(jnp.float32), axis=1
    ).reshape(slots, width)
    mix_rows = jnp.sum(
        (pick_pairs.astype(jnp.float32) * expert_weights.reshape(-1)[None, :]).reshape(slots, tokens, TOPK),
        axis=2,
    )
    addition = jnp.einsum("st,sd->td", mix_rows, per_expert, precision=lax.Precision.HIGHEST)
    return (summed + addition).astype(jnp.bfloat16)


def solution(mesh):
    fine = Mesh(mesh.devices.reshape(4, 2, 2, 4, 4, 2), (*DP, *TENSOR))
    in_specs = (
        P(DP, TENSOR),
        P(DP, TENSOR),
        P(DP, None, TENSOR),
        P(DP, None, TENSOR),
        P(DP),
        P(TENSOR),
        P(DP, None),
        P(DP, None),
        P(TENSOR, DP),
        P(DP, TENSOR),
    )
    return jax.shard_map(shards, mesh=fine, in_specs=in_specs, out_specs=P(DP, TENSOR), check_vma=False)
```

```python
import jax
import jax.numpy as jnp
from jax import lax
from jax.experimental import pallas as pl
from jax.experimental.pallas import tpu as pltpu
from jax.sharding import Mesh, PartitionSpec as P

HEADS = 48
KV = 8
HEAD = 128
D = 6144
EXPERTS = 8
TOPK = 2
CACHE = 128
SRC_CAP = 16
BLOCKS = 64
CLASSES = 4
PER_CLASS = SRC_CAP // CLASSES
CAPACITY = 384
CLASS_ROWS = CAPACITY // CLASSES + BLOCKS * 6 // (4 * CLASSES)
META = 128
ROWS = CLASSES * CLASS_ROWS
SQUARES = 16
UNIT = 128

NORM_EPSILON = 1e-05

DP = ("x", "zh", "zq", "zn")
TENSOR = ("y", "core")


def attend(residual, queries, keys, values, lengths):
    tokens, width = residual.shape
    group_size = HEADS // KV
    query_rows = queries.reshape(tokens, group_size, HEAD)
    scores = jnp.einsum(
        "tjd,tld->tjl", query_rows, keys, preferred_element_type=jnp.float32
    ) * HEAD ** (-0.5)
    live_mask = (jnp.arange(CACHE, dtype=jnp.int32)[None, :] < lengths[:, None])[:, None, :]
    scores = jnp.where(live_mask, scores, -1e30)
    peak_score = jnp.max(scores, axis=-1, keepdims=True)
    powered = jnp.exp(scores - peak_score)
    probs = (powered / jnp.sum(powered, axis=-1, keepdims=True)).astype(jnp.bfloat16)
    attended = jnp.einsum("tjl,tld->tjd", probs, values, preferred_element_type=jnp.float32)
    return residual.astype(jnp.float32) + attended.reshape(tokens, width)


def summed_at_owner(pieces, axis):
    return jnp.sum(
        lax.all_to_all(pieces, axis, split_axis=0, concat_axis=0, tiled=True).astype(jnp.float32), axis=0
    )


def diagonal():
    row = lax.broadcasted_iota(jnp.int32, (CLASS_ROWS, UNIT), 0)
    return row == lax.broadcasted_iota(jnp.int32, (CLASS_ROWS, UNIT), 1)


def leading_and_rest(sums):
    leading = sums.astype(jnp.bfloat16)
    return jnp.concatenate([leading, (sums - leading.astype(jnp.float32)).astype(jnp.bfloat16)], axis=0)


def hidden_kernel(core_ref, rows_ref, gain_ref, w_ref, send_ref, keep_ref, scaled_ref, squares_ref):
    step = pl.program_id(0)

    @pl.when(step == 0)
    def _():
        wide = rows_ref[...].astype(jnp.float32)
        scaled_ref[...] = (wide * gain_ref[...].astype(jnp.float32)).astype(jnp.bfloat16)
        sums = jnp.sum(wide * wide, axis=1, keepdims=True)
        lines = [
            jnp.sum(
                jnp.where(diagonal(), sums[c * CLASS_ROWS : (c + 1) * CLASS_ROWS], 0.0),
                axis=0,
                keepdims=True,
            )
            for c in range(CLASSES)
        ]
        lines.append(jnp.zeros((SQUARES // 2 - CLASSES, UNIT), jnp.float32))
        squares_ref[...] = leading_and_rest(jnp.concatenate(lines, axis=0))

    sums = jnp.dot(scaled_ref[...], w_ref[...], preferred_element_type=jnp.float32)

    def write(out_ref):
        for half in range(2):
            out_ref[half, :ROWS] = sums[:, half * UNIT : (half + 1) * UNIT].astype(jnp.bfloat16)
            out_ref[half, ROWS:] = squares_ref[...]

    @pl.when(step < 2)
    def _():
        write(send_ref)

    @pl.when(step >= 2)
    def _():
        write(keep_ref)


def hidden_pieces(rows, norm_gain, w_in, core):
    width, units = w_in.shape
    half = jax.ShapeDtypeStruct((units // (2 * UNIT), ROWS + SQUARES, UNIT), jnp.bfloat16)
    block = (2, ROWS + SQUARES, UNIT)
    return pl.pallas_call(
        hidden_kernel,
        grid_spec=pltpu.PrefetchScalarGridSpec(
            num_scalar_prefetch=1,
            grid=(4,),
            in_specs=[
                pl.BlockSpec((ROWS, width), lambda i, c: (0, 0)),
                pl.BlockSpec((1, width), lambda i, c: (0, 0)),
                pl.BlockSpec((width, 2 * UNIT), lambda i, c: (0, (i + 2 - 2 * c[0]) % 4)),
            ],
            out_specs=[
                pl.BlockSpec(block, lambda i, c: (jnp.minimum(i, 1), 0, 0)),
                pl.BlockSpec(block, lambda i, c: (jnp.maximum(i - 2, 0), 0, 0)),
            ],
            scratch_shapes=[
                pltpu.VMEM((ROWS, width), jnp.bfloat16),
                pltpu.VMEM((SQUARES, UNIT), jnp.bfloat16),
            ],
        ),
        out_shape=[half, half],
        compiler_params=pltpu.CompilerParams(vmem_limit_bytes=32 << 20),
        name="hidden_pieces",
    )(core.reshape(1), rows, norm_gain.reshape(1, width), pltpu.with_memory_space_constraint(w_in, pltpu.HBM))


def core_kernel(own_ref, other_ref, out_ref):
    out_ref[:, :ROWS] = (
        own_ref[:, :ROWS].astype(jnp.float32) + other_ref[:, :ROWS].astype(jnp.float32)
    ).astype(jnp.bfloat16)
    both = own_ref[0, ROWS:].astype(jnp.float32) + other_ref[0, ROWS:].astype(jnp.float32)
    split = leading_and_rest(both[: SQUARES // 2] + both[SQUARES // 2 :])
    for piece in range(out_ref.shape[0]):
        out_ref[piece, ROWS:] = split


def core_summed(own, other):
    return pl.pallas_call(
        core_kernel,
        out_shape=jax.ShapeDtypeStruct(own.shape, jnp.bfloat16),
        compiler_params=pltpu.CompilerParams(vmem_limit_bytes=32 << 20),
        name="core_summed",
    )(own, other)


def silu_kernel(in_ref, out_ref):
    total = in_ref[0].astype(jnp.float32)
    for piece in range(1, in_ref.shape[0]):
        total = total + in_ref[piece].astype(jnp.float32)
    squares = total[ROWS : ROWS + SQUARES // 2] + total[ROWS + SQUARES // 2 :]
    for c in range(CLASSES):
        own = jnp.sum(jnp.where(diagonal(), squares[c : c + 1], 0.0), axis=1, keepdims=True)
        scaled = total[c * CLASS_ROWS : (c + 1) * CLASS_ROWS] * lax.rsqrt(own / D + NORM_EPSILON)
        hidden = (scaled / (1.0 + jnp.exp(-scaled))).astype(jnp.bfloat16)
        for piece in range(out_ref.shape[0]):
            out_ref[piece, c * CLASS_ROWS : (c + 1) * CLASS_ROWS] = hidden


def silu_copies(pieces):
    return pl.pallas_call(
        silu_kernel,
        out_shape=jax.ShapeDtypeStruct((pieces.shape[0], ROWS, UNIT), jnp.bfloat16),
        compiler_params=pltpu.CompilerParams(vmem_limit_bytes=32 << 20),
        name="silu_copies",
    )(pieces)


def compact_kernel(class_ref, received_ref, rows_ref, place_ref):
    slots = received_ref.shape[0]
    width = rows_ref.shape[1]
    own_class = class_ref[0]
    row = lax.broadcasted_iota(jnp.int32, (slots, slots), 0)
    column = lax.broadcasted_iota(jnp.int32, (slots, slots), 1)
    earlier = (column // PER_CLASS < row // PER_CLASS) & (column % PER_CLASS == 0)
    earlier = earlier.astype(jnp.float32).astype(jnp.bfloat16)

    def earlier_sum(counts):
        return jnp.dot(earlier, counts, preferred_element_type=jnp.float32).astype(jnp.int32)

    counts = received_ref[:, width:]
    named = counts.astype(jnp.float32).astype(jnp.int32)
    kept = jnp.clip(CAPACITY - earlier_sum(counts), 0, named)
    line = lax.broadcasted_iota(jnp.int32, named.shape, 0)
    block, place = line // PER_CLASS, line % PER_CLASS
    shift = (own_class + BLOCKS - block) % CLASSES
    in_class = (kept - shift + CLASSES - 1) // CLASSES
    first = earlier_sum(in_class.astype(jnp.float32).astype(jnp.bfloat16))
    spot = jnp.where(place < in_class, first + place, -1)
    chosen = spot == lax.broadcasted_iota(jnp.int32, named.shape, 1)
    chosen = chosen.astype(jnp.float32).astype(jnp.bfloat16)
    place_ref[...] = chosen
    rows = lax.dot_general(
        chosen, received_ref[:, :width], (((0,), (0,)), ((), ())), preferred_element_type=jnp.float32
    )
    rows_ref[...] = rows[: rows_ref.shape[0]].astype(jnp.bfloat16)


def compacted(received, own_class):
    slots, wide = received.shape
    return pl.pallas_call(
        compact_kernel,
        in_specs=[
            pl.BlockSpec(memory_space=pltpu.SMEM),
            pl.BlockSpec(memory_space=pltpu.VMEM),
        ],
        out_shape=[
            jax.ShapeDtypeStruct((CLASS_ROWS, wide - META), jnp.bfloat16),
            jax.ShapeDtypeStruct((slots, META), jnp.bfloat16),
        ],
        compiler_params=pltpu.CompilerParams(vmem_limit_bytes=32 << 20),
        name="compacted",
    )(own_class.reshape(1), received)


def shards(
    residual, queries, keys, values, lengths, norm_gain, expert_ids, expert_weights, w_in, w_out
):
    tokens, width = residual.shape
    block = ((lax.axis_index("x") * 2 + lax.axis_index("zh")) * 2 + lax.axis_index("zq")) * 4 + lax.axis_index("zn")
    own_class = lax.axis_index("zn")

    summed = attend(residual, queries, keys, values, lengths)
    unscaled = summed.astype(jnp.bfloat16)

    flat_ids = expert_ids.reshape(-1)
    pairs = flat_ids.shape[0]
    same = flat_ids[:, None] == flat_ids[None, :]
    earlier = jnp.arange(pairs)[:, None] > jnp.arange(pairs)[None, :]
    rank = jnp.sum((same & earlier).astype(jnp.int32), axis=1)
    slots = EXPERTS * SRC_CAP
    target = flat_ids * SRC_CAP + (rank + block) % CLASSES * PER_CLASS + rank // CLASSES
    pick_pairs = target[None, :] == jnp.arange(slots, dtype=jnp.int32)[:, None]
    pick_tokens = jnp.sum(
        pick_pairs.reshape(slots, tokens, TOPK).astype(jnp.float32), axis=2
    ).astype(jnp.bfloat16)
    counts = jnp.sum(
        (flat_ids[None, :] == jnp.arange(EXPERTS, dtype=jnp.int32)[:, None]).astype(jnp.float32), axis=1
    ).astype(jnp.bfloat16)

    packed = jnp.dot(pick_tokens, unscaled, preferred_element_type=jnp.float32).astype(jnp.bfloat16)
    packed = packed.reshape(EXPERTS, 1, CLASSES, PER_CLASS, width)
    meta = jnp.broadcast_to(counts[:, None, None, None, None], (EXPERTS, 1, CLASSES, PER_CLASS, META))
    outgoing = jnp.concatenate([packed, meta], axis=-1)
    outgoing = jnp.broadcast_to(outgoing, (EXPERTS, 2, CLASSES, PER_CLASS, width + META))
    received = lax.all_to_all(
        outgoing.reshape(BLOCKS, PER_CLASS, width + META), DP, split_axis=0, concat_axis=0, tiled=True
    )

    class_rows, chosen = compacted(received.reshape(BLOCKS * PER_CLASS, width + META), own_class)
    rows = lax.all_gather(class_rows, "zn", axis=0, tiled=True)
    send, own = hidden_pieces(rows, norm_gain, w_in, lax.axis_index("core"))
    other = lax.ppermute(send, "core", ((0, 1), (1, 0)))
    pieces = lax.all_to_all(core_summed(own, other), "y", split_axis=0, concat_axis=0, tiled=True)
    gathered = lax.all_to_all(silu_copies(pieces), "y", split_axis=0, concat_axis=0, tiled=True)
    gathered = lax.all_gather(gathered, "core", axis=0, tiled=True)
    hidden = jnp.moveaxis(gathered, 0, 1).reshape(ROWS, 8 * UNIT)
    results = jnp.dot(hidden, w_out, preferred_element_type=jnp.float32).astype(jnp.bfloat16)

    class_out = summed_at_owner(results.reshape(CLASSES, CLASS_ROWS, width), "zn").astype(jnp.bfloat16)
    returned = jnp.dot(
        chosen[:, :CLASS_ROWS], class_out, preferred_element_type=jnp.float32
    ).astype(jnp.bfloat16)
    combined = lax.all_to_all(
        returned.reshape(BLOCKS, PER_CLASS, width), DP, split_axis=0, concat_axis=0, tiled=True
    )
    per_expert = jnp.sum(
        combined.reshape(EXPERTS, 2, SRC_CAP, width).astype(jnp.float32), axis=1
    ).reshape(slots, width)
    mix_rows = jnp.sum(
        (pick_pairs.astype(jnp.float32) * expert_weights.reshape(-1)[None, :]).reshape(slots, tokens, TOPK),
        axis=2,
    )
    addition = jnp.einsum("st,sd->td", mix_rows, per_expert, precision=lax.Precision.HIGHEST)
    return (summed + addition).astype(jnp.bfloat16)


def solution(mesh):
    fine = Mesh(mesh.devices.reshape(4, 2, 2, 4, 4, 2), (*DP, *TENSOR))
    in_specs = (
        P(DP, TENSOR),
        P(DP, TENSOR),
        P(DP, None, TENSOR),
        P(DP, None, TENSOR),
        P(DP),
        P(TENSOR),
        P(DP, None),
        P(DP, None),
        P(TENSOR, DP),
        P(DP, TENSOR),
    )
    return jax.shard_map(shards, mesh=fine, in_specs=in_specs, out_specs=P(DP, TENSOR), check_vma=False)
```

```python
import jax
import jax.numpy as jnp
from jax import lax
from jax.experimental import pallas as pl
from jax.experimental.pallas import tpu as pltpu
from jax.sharding import Mesh, PartitionSpec as P

HEADS = 48
KV = 8
HEAD = 128
D = 6144
EXPERTS = 8
TOPK = 2
CACHE = 128
SRC_CAP = 16
BLOCKS = 64
CLASSES = 4
PER_CLASS = SRC_CAP // CLASSES
CAPACITY = 384
CLASS_ROWS = CAPACITY // CLASSES + BLOCKS * 6 // (4 * CLASSES)
META = 128
ROWS = CLASSES * CLASS_ROWS
SQUARES = 16
UNIT = 128

NORM_EPSILON = 1e-05

DP = ("x", "zh", "zq", "zn")
TENSOR = ("y", "core")


TOKENS = 32
STEP = 16
GROUP = HEADS // KV


def route(block, ids_ref, weights_ref):
    ids = ids_ref[...]
    experts = lax.broadcasted_iota(jnp.int32, (EXPERTS, TOKENS), 0)
    names = [(ids[k : k + 1] == experts).astype(jnp.float32) for k in range(TOPK)]
    named = names[0] + names[1]
    before = lax.broadcasted_iota(jnp.int32, (TOKENS, TOKENS), 0) < lax.broadcasted_iota(
        jnp.int32, (TOKENS, TOKENS), 1
    )
    earlier = jnp.dot(named, before.astype(jnp.float32), preferred_element_type=jnp.float32)
    slot = lax.broadcasted_iota(jnp.int32, (EXPERTS * SRC_CAP, TOKENS), 0)
    pick = jnp.zeros(slot.shape, jnp.float32)
    mix = jnp.zeros(slot.shape, jnp.float32)
    for k in range(TOPK):
        rank = jnp.sum(earlier * names[k], axis=0, keepdims=True).astype(jnp.int32)
        target = ids[k : k + 1] * SRC_CAP + (rank + block) % CLASSES * PER_CLASS + rank // CLASSES
        here = slot == target
        pick = jnp.where(here, 1.0, pick)
        mix = jnp.where(here, weights_ref[k : k + 1], mix)
    return pick, mix, jnp.sum(named, axis=1, keepdims=True)


def tokens_kernel(
    block_ref, lengths_ref, ids_ref, weights_ref, residual_ref, queries_ref, keys_ref, values_ref,
    summed_ref, out_ref, mix_ref, query_ref, attended_ref, all_ref,
):
    step = pl.program_id(0)

    @pl.when(step == 0)
    def _():
        query_ref[...] = jnp.zeros_like(query_ref)

    for h in range(GROUP):
        query_ref[:, h, :] = queries_ref[:, h * HEAD : (h + 1) * HEAD].astype(jnp.float32)
    position = lax.broadcasted_iota(jnp.int32, (8, CACHE), 1)
    for t in range(STEP):
        scores = lax.dot_general(
            query_ref[t].astype(jnp.bfloat16),
            keys_ref[t],
            (((1,), (1,)), ((), ())),
            preferred_element_type=jnp.float32,
        ) * HEAD ** (-0.5)
        scores = jnp.where(position < lengths_ref[step * STEP + t], scores, -1e30)
        powered = jnp.exp(scores - jnp.max(scores, axis=1, keepdims=True))
        probs = (powered / jnp.sum(powered, axis=1, keepdims=True)).astype(jnp.bfloat16)
        attended_ref[t] = jnp.dot(probs, values_ref[t], preferred_element_type=jnp.float32)
    for h in range(GROUP):
        lanes = slice(h * HEAD, (h + 1) * HEAD)
        total = residual_ref[:, lanes].astype(jnp.float32) + attended_ref[:, h, :]
        summed_ref[:, lanes] = total
        all_ref[pl.ds(pl.multiple_of(step * STEP, STEP), STEP), lanes] = total

    @pl.when(step == TOKENS // STEP - 1)
    def _():
        pick, mix, counts = route(block_ref[0], ids_ref, weights_ref)
        mix_ref[...] = mix
        packed = jnp.dot(
            pick.astype(jnp.bfloat16), all_ref[...].astype(jnp.bfloat16), preferred_element_type=jnp.float32
        )
        width = packed.shape[1]
        for e in range(EXPERTS):
            meta = jnp.broadcast_to(counts[e : e + 1], (PER_CLASS, META)).astype(jnp.bfloat16)
            for c in range(CLASSES):
                first = e * SRC_CAP + c * PER_CLASS
                rows = packed[first : first + PER_CLASS].astype(jnp.bfloat16)
                for group in range(2):
                    peer = (e * 2 + group) * CLASSES + c
                    out_ref[peer, :, :width] = rows
                    out_ref[peer, :, width:] = meta


def tokens_packed(block, lengths, expert_ids, expert_weights, residual, queries, keys, values):
    tokens, width = residual.shape
    whole = lambda *shape: pl.BlockSpec(shape, lambda i: (0,) * len(shape))
    return pl.pallas_call(
        tokens_kernel,
        grid=(TOKENS // STEP,),
        in_specs=[
            pl.BlockSpec(memory_space=pltpu.SMEM),
            pl.BlockSpec(memory_space=pltpu.SMEM),
            whole(TOPK, TOKENS),
            whole(TOPK, TOKENS),
            pl.BlockSpec((STEP, width), lambda i: (i, 0)),
            pl.BlockSpec((STEP, width), lambda i: (i, 0)),
            pl.BlockSpec((STEP, CACHE, HEAD), lambda i: (i, 0, 0)),
            pl.BlockSpec((STEP, CACHE, HEAD), lambda i: (i, 0, 0)),
        ],
        out_specs=[
            pl.BlockSpec((STEP, width), lambda i: (i, 0)),
            whole(BLOCKS, PER_CLASS, width + META),
            whole(EXPERTS * SRC_CAP, TOKENS),
        ],
        out_shape=[
            jax.ShapeDtypeStruct((tokens, width), jnp.float32),
            jax.ShapeDtypeStruct((BLOCKS, PER_CLASS, width + META), jnp.bfloat16),
            jax.ShapeDtypeStruct((EXPERTS * SRC_CAP, TOKENS), jnp.float32),
        ],
        scratch_shapes=[
            pltpu.VMEM((STEP, 8, HEAD), jnp.float32),
            pltpu.VMEM((STEP, 8, HEAD), jnp.float32),
            pltpu.VMEM((TOKENS, width), jnp.float32),
        ],
        compiler_params=pltpu.CompilerParams(vmem_limit_bytes=32 << 20),
        name="tokens_packed",
    )(
        block.reshape(1),
        *(
            pltpu.with_memory_space_constraint(operand, pltpu.HBM)
            for operand in (lengths, expert_ids.T, expert_weights.T, residual, queries, keys, values)
        ),
    )


def summed_at_owner(pieces, axis):
    return jnp.sum(
        lax.all_to_all(pieces, axis, split_axis=0, concat_axis=0, tiled=True).astype(jnp.float32), axis=0
    )


def diagonal():
    row = lax.broadcasted_iota(jnp.int32, (CLASS_ROWS, UNIT), 0)
    return row == lax.broadcasted_iota(jnp.int32, (CLASS_ROWS, UNIT), 1)


def leading_and_rest(sums):
    leading = sums.astype(jnp.bfloat16)
    return jnp.concatenate([leading, (sums - leading.astype(jnp.float32)).astype(jnp.bfloat16)], axis=0)


def hidden_kernel(core_ref, rows_ref, gain_ref, w_ref, send_ref, keep_ref, held_ref, sems):
    columns = 2 * UNIT
    copies = []
    for k in range(4):
        source = (k + 2 - 2 * core_ref[0]) % 4 * columns
        copies.append(
            pltpu.make_async_copy(
                w_ref.at[:, pl.ds(pl.multiple_of(source, columns), columns)], held_ref.at[k], sems.at[k]
            )
        )
        copies[k].start()

    wide = rows_ref[...].astype(jnp.float32)
    scaled = (wide * gain_ref[...].astype(jnp.float32)).astype(jnp.bfloat16)
    sums = jnp.sum(wide * wide, axis=1, keepdims=True)
    lines = [
        jnp.sum(
            jnp.where(diagonal(), sums[c * CLASS_ROWS : (c + 1) * CLASS_ROWS], 0.0), axis=0, keepdims=True
        )
        for c in range(CLASSES)
    ]
    lines.append(jnp.zeros((SQUARES // 2 - CLASSES, UNIT), jnp.float32))
    squares = leading_and_rest(jnp.concatenate(lines, axis=0))

    for k in range(4):
        out_ref = send_ref if k < 2 else keep_ref
        copies[k].wait()
        parts = jnp.dot(scaled, held_ref[k], preferred_element_type=jnp.float32)
        for half in range(2):
            piece = k % 2 * 2 + half
            out_ref[piece, :ROWS] = parts[:, half * UNIT : (half + 1) * UNIT].astype(jnp.bfloat16)
            out_ref[piece, ROWS:] = squares


def hidden_pieces(rows, norm_gain, w_in, core):
    width, units = w_in.shape
    half = jax.ShapeDtypeStruct((units // (2 * UNIT), ROWS + SQUARES, UNIT), jnp.bfloat16)
    return pl.pallas_call(
        hidden_kernel,
        in_specs=[
            pl.BlockSpec(memory_space=pltpu.SMEM),
            pl.BlockSpec(memory_space=pltpu.VMEM),
            pl.BlockSpec(memory_space=pltpu.VMEM),
            pl.BlockSpec(memory_space=pl.ANY),
        ],
        out_shape=[half, half],
        scratch_shapes=[
            pltpu.VMEM((4, width, 2 * UNIT), jnp.bfloat16),
            pltpu.SemaphoreType.DMA((4,)),
        ],
        compiler_params=pltpu.CompilerParams(vmem_limit_bytes=32 << 20),
        name="hidden_pieces",
    )(core.reshape(1), rows, norm_gain.reshape(1, width), pltpu.with_memory_space_constraint(w_in, pltpu.HBM))


def core_kernel(own_ref, other_ref, out_ref):
    out_ref[:, :ROWS] = (
        own_ref[:, :ROWS].astype(jnp.float32) + other_ref[:, :ROWS].astype(jnp.float32)
    ).astype(jnp.bfloat16)
    both = own_ref[0, ROWS:].astype(jnp.float32) + other_ref[0, ROWS:].astype(jnp.float32)
    split = leading_and_rest(both[: SQUARES // 2] + both[SQUARES // 2 :])
    for piece in range(out_ref.shape[0]):
        out_ref[piece, ROWS:] = split


def core_summed(own, other):
    return pl.pallas_call(
        core_kernel,
        out_shape=jax.ShapeDtypeStruct(own.shape, jnp.bfloat16),
        compiler_params=pltpu.CompilerParams(vmem_limit_bytes=32 << 20),
        name="core_summed",
    )(own, other)


def silu_kernel(in_ref, out_ref):
    total = in_ref[0].astype(jnp.float32)
    for piece in range(1, in_ref.shape[0]):
        total = total + in_ref[piece].astype(jnp.float32)
    squares = total[ROWS : ROWS + SQUARES // 2] + total[ROWS + SQUARES // 2 :]
    for c in range(CLASSES):
        own = jnp.sum(jnp.where(diagonal(), squares[c : c + 1], 0.0), axis=1, keepdims=True)
        scaled = total[c * CLASS_ROWS : (c + 1) * CLASS_ROWS] * lax.rsqrt(own / D + NORM_EPSILON)
        hidden = (scaled / (1.0 + jnp.exp(-scaled))).astype(jnp.bfloat16)
        for piece in range(out_ref.shape[0]):
            out_ref[piece, c * CLASS_ROWS : (c + 1) * CLASS_ROWS] = hidden


def silu_copies(pieces):
    return pl.pallas_call(
        silu_kernel,
        out_shape=jax.ShapeDtypeStruct((pieces.shape[0], ROWS, UNIT), jnp.bfloat16),
        compiler_params=pltpu.CompilerParams(vmem_limit_bytes=32 << 20),
        name="silu_copies",
    )(pieces)


def compact_kernel(class_ref, received_ref, rows_ref, place_ref):
    slots = received_ref.shape[0]
    width = rows_ref.shape[1]
    own_class = class_ref[0]
    row = lax.broadcasted_iota(jnp.int32, (slots, slots), 0)
    column = lax.broadcasted_iota(jnp.int32, (slots, slots), 1)
    earlier = (column // PER_CLASS < row // PER_CLASS) & (column % PER_CLASS == 0)
    earlier = earlier.astype(jnp.float32).astype(jnp.bfloat16)

    def earlier_sum(counts):
        return jnp.dot(earlier, counts, preferred_element_type=jnp.float32).astype(jnp.int32)

    counts = received_ref[:, width:]
    named = counts.astype(jnp.float32).astype(jnp.int32)
    kept = jnp.clip(CAPACITY - earlier_sum(counts), 0, named)
    line = lax.broadcasted_iota(jnp.int32, named.shape, 0)
    block, place = line // PER_CLASS, line % PER_CLASS
    shift = (own_class + BLOCKS - block) % CLASSES
    in_class = (kept - shift + CLASSES - 1) // CLASSES
    first = earlier_sum(in_class.astype(jnp.float32).astype(jnp.bfloat16))
    spot = jnp.where(place < in_class, first + place, -1)
    chosen = spot == lax.broadcasted_iota(jnp.int32, named.shape, 1)
    chosen = chosen.astype(jnp.float32).astype(jnp.bfloat16)
    place_ref[...] = chosen
    rows = lax.dot_general(
        chosen, received_ref[:, :width], (((0,), (0,)), ((), ())), preferred_element_type=jnp.float32
    )
    rows_ref[...] = rows[: rows_ref.shape[0]].astype(jnp.bfloat16)


def compacted(received, own_class):
    slots, wide = received.shape
    return pl.pallas_call(
        compact_kernel,
        in_specs=[
            pl.BlockSpec(memory_space=pltpu.SMEM),
            pl.BlockSpec(memory_space=pltpu.VMEM),
        ],
        out_shape=[
            jax.ShapeDtypeStruct((CLASS_ROWS, wide - META), jnp.bfloat16),
            jax.ShapeDtypeStruct((slots, META), jnp.bfloat16),
        ],
        compiler_params=pltpu.CompilerParams(vmem_limit_bytes=32 << 20),
        name="compacted",
    )(own_class.reshape(1), received)


def shards(
    residual, queries, keys, values, lengths, norm_gain, expert_ids, expert_weights, w_in, w_out
):
    tokens, width = residual.shape
    block = ((lax.axis_index("x") * 2 + lax.axis_index("zh")) * 2 + lax.axis_index("zq")) * 4 + lax.axis_index("zn")
    own_class = lax.axis_index("zn")

    summed, outgoing, mix_rows = tokens_packed(
        block, lengths, expert_ids, expert_weights, residual, queries, keys, values
    )
    received = lax.all_to_all(outgoing, DP, split_axis=0, concat_axis=0, tiled=True)
    class_rows, chosen = compacted(received.reshape(BLOCKS * PER_CLASS, width + META), own_class)
    rows = lax.all_gather(class_rows, "zn", axis=0, tiled=True)
    send, own = hidden_pieces(rows, norm_gain, w_in, lax.axis_index("core"))
    other = lax.ppermute(send, "core", ((0, 1), (1, 0)))
    pieces = lax.all_to_all(core_summed(own, other), "y", split_axis=0, concat_axis=0, tiled=True)
    gathered = lax.all_to_all(silu_copies(pieces), "y", split_axis=0, concat_axis=0, tiled=True)
    gathered = lax.all_gather(gathered, "core", axis=0, tiled=True)
    hidden = jnp.moveaxis(gathered, 0, 1).reshape(ROWS, 8 * UNIT)
    results = jnp.dot(hidden, w_out, preferred_element_type=jnp.float32).astype(jnp.bfloat16)

    class_out = summed_at_owner(results.reshape(CLASSES, CLASS_ROWS, width), "zn").astype(jnp.bfloat16)
    returned = jnp.dot(
        chosen[:, :CLASS_ROWS], class_out, preferred_element_type=jnp.float32
    ).astype(jnp.bfloat16)
    combined = lax.all_to_all(
        returned.reshape(BLOCKS, PER_CLASS, width), DP, split_axis=0, concat_axis=0, tiled=True
    )
    per_expert = jnp.sum(
        combined.reshape(EXPERTS, 2, SRC_CAP, width).astype(jnp.float32), axis=1
    ).reshape(EXPERTS * SRC_CAP, width)
    addition = jnp.einsum("st,sd->td", mix_rows, per_expert, precision=lax.Precision.HIGHEST)
    return (summed + addition).astype(jnp.bfloat16)


def solution(mesh):
    fine = Mesh(mesh.devices.reshape(4, 2, 2, 4, 4, 2), (*DP, *TENSOR))
    in_specs = (
        P(DP, TENSOR),
        P(DP, TENSOR),
        P(DP, None, TENSOR),
        P(DP, None, TENSOR),
        P(DP),
        P(TENSOR),
        P(DP, None),
        P(DP, None),
        P(TENSOR, DP),
        P(DP, TENSOR),
    )
    return jax.shard_map(shards, mesh=fine, in_specs=in_specs, out_specs=P(DP, TENSOR), check_vma=False)
```

```python
import jax
import jax.numpy as jnp
from jax import lax
from jax.experimental import pallas as pl
from jax.experimental.pallas import tpu as pltpu
from jax.sharding import Mesh, PartitionSpec as P

HEADS = 48
KV = 8
HEAD = 128
D = 6144
EXPERTS = 8
TOPK = 2
CACHE = 128
SRC_CAP = 16
BLOCKS = 64
CLASSES = 4
PER_CLASS = SRC_CAP // CLASSES
CAPACITY = 384
CLASS_ROWS = CAPACITY // CLASSES + BLOCKS * 6 // (4 * CLASSES)
META = 128
ROWS = CLASSES * CLASS_ROWS
SQUARES = 16
UNIT = 128

NORM_EPSILON = 1e-05

DP = ("x", "zh", "zq", "zn")
TENSOR = ("y", "core")


TOKENS = 32
STEP = 32
GROUP = HEADS // KV


def route(block, ids_ref, weights_ref):
    ids = ids_ref[...]
    experts = lax.broadcasted_iota(jnp.int32, (EXPERTS, TOKENS), 0)
    names = [(ids[k : k + 1] == experts).astype(jnp.float32) for k in range(TOPK)]
    named = names[0] + names[1]
    before = lax.broadcasted_iota(jnp.int32, (TOKENS, TOKENS), 0) < lax.broadcasted_iota(
        jnp.int32, (TOKENS, TOKENS), 1
    )
    earlier = jnp.dot(named, before.astype(jnp.float32), preferred_element_type=jnp.float32)
    slot = lax.broadcasted_iota(jnp.int32, (EXPERTS * SRC_CAP, TOKENS), 0)
    pick = jnp.zeros(slot.shape, jnp.float32)
    mix = jnp.zeros(slot.shape, jnp.float32)
    for k in range(TOPK):
        rank = jnp.sum(earlier * names[k], axis=0, keepdims=True).astype(jnp.int32)
        target = ids[k : k + 1] * SRC_CAP + (rank + block) % CLASSES * PER_CLASS + rank // CLASSES
        here = slot == target
        pick = jnp.where(here, 1.0, pick)
        mix = jnp.where(here, weights_ref[k : k + 1], mix)
    return pick, mix, jnp.sum(named, axis=1, keepdims=True)


def tokens_kernel(
    block_ref, lengths_ref, ids_ref, weights_ref, residual_ref, queries_ref, keys_ref, values_ref,
    summed_ref, out_ref, mix_ref, query_ref, attended_ref, all_ref,
):
    step = pl.program_id(0)

    @pl.when(step == 0)
    def _():
        query_ref[...] = jnp.zeros_like(query_ref)

    for h in range(GROUP):
        query_ref[:, h, :] = queries_ref[:, h * HEAD : (h + 1) * HEAD].astype(jnp.float32)
    position = lax.broadcasted_iota(jnp.int32, (8, CACHE), 1)
    scores = []
    for t in range(STEP):
        products = lax.dot_general(
            query_ref[t].astype(jnp.bfloat16),
            keys_ref[t],
            (((1,), (1,)), ((), ())),
            preferred_element_type=jnp.float32,
        ) * HEAD ** (-0.5)
        scores.append(jnp.where(position < lengths_ref[step * STEP + t], products, -1e30))
    scores = jnp.concatenate(scores, axis=0)
    powered = jnp.exp(scores - jnp.max(scores, axis=1, keepdims=True))
    probs = powered / jnp.sum(powered, axis=1, keepdims=True)
    for t in range(STEP):
        attended_ref[t] = jnp.dot(
            probs[t * 8 : (t + 1) * 8].astype(jnp.bfloat16), values_ref[t], preferred_element_type=jnp.float32
        )
    for h in range(GROUP):
        lanes = slice(h * HEAD, (h + 1) * HEAD)
        total = residual_ref[:, lanes].astype(jnp.float32) + attended_ref[:, h, :]
        summed_ref[:, lanes] = total
        all_ref[pl.ds(pl.multiple_of(step * STEP, STEP), STEP), lanes] = total

    @pl.when(step == TOKENS // STEP - 1)
    def _():
        pick, mix, counts = route(block_ref[0], ids_ref, weights_ref)
        mix_ref[...] = mix
        packed = jnp.dot(
            pick.astype(jnp.bfloat16), all_ref[...].astype(jnp.bfloat16), preferred_element_type=jnp.float32
        )
        width = packed.shape[1]
        for e in range(EXPERTS):
            meta = jnp.broadcast_to(counts[e : e + 1], (PER_CLASS, META)).astype(jnp.bfloat16)
            for c in range(CLASSES):
                first = e * SRC_CAP + c * PER_CLASS
                rows = packed[first : first + PER_CLASS].astype(jnp.bfloat16)
                for group in range(2):
                    peer = (e * 2 + group) * CLASSES + c
                    out_ref[peer, :, :width] = rows
                    out_ref[peer, :, width:] = meta


def tokens_packed(block, lengths, expert_ids, expert_weights, residual, queries, keys, values):
    tokens, width = residual.shape
    whole = lambda *shape: pl.BlockSpec(shape, lambda i: (0,) * len(shape))
    return pl.pallas_call(
        tokens_kernel,
        grid=(TOKENS // STEP,),
        in_specs=[
            pl.BlockSpec(memory_space=pltpu.SMEM),
            pl.BlockSpec(memory_space=pltpu.SMEM),
            whole(TOPK, TOKENS),
            whole(TOPK, TOKENS),
            pl.BlockSpec((STEP, width), lambda i: (i, 0)),
            pl.BlockSpec((STEP, width), lambda i: (i, 0)),
            pl.BlockSpec((STEP, CACHE, HEAD), lambda i: (i, 0, 0)),
            pl.BlockSpec((STEP, CACHE, HEAD), lambda i: (i, 0, 0)),
        ],
        out_specs=[
            pl.BlockSpec((STEP, width), lambda i: (i, 0)),
            whole(BLOCKS, PER_CLASS, width + META),
            whole(EXPERTS * SRC_CAP, TOKENS),
        ],
        out_shape=[
            jax.ShapeDtypeStruct((tokens, width), jnp.float32),
            jax.ShapeDtypeStruct((BLOCKS, PER_CLASS, width + META), jnp.bfloat16),
            jax.ShapeDtypeStruct((EXPERTS * SRC_CAP, TOKENS), jnp.float32),
        ],
        scratch_shapes=[
            pltpu.VMEM((STEP, 8, HEAD), jnp.float32),
            pltpu.VMEM((STEP, 8, HEAD), jnp.float32),
            pltpu.VMEM((TOKENS, width), jnp.float32),
        ],
        compiler_params=pltpu.CompilerParams(vmem_limit_bytes=10 << 20),
        name="tokens_packed",
    )(
        block.reshape(1),
        *(
            pltpu.with_memory_space_constraint(operand, pltpu.HBM)
            for operand in (lengths, expert_ids.T, expert_weights.T, residual, queries, keys, values)
        ),
    )


def summed_at_owner(pieces, axis):
    return jnp.sum(
        lax.all_to_all(pieces, axis, split_axis=0, concat_axis=0, tiled=True).astype(jnp.float32), axis=0
    )


def diagonal():
    row = lax.broadcasted_iota(jnp.int32, (CLASS_ROWS, UNIT), 0)
    return row == lax.broadcasted_iota(jnp.int32, (CLASS_ROWS, UNIT), 1)


def leading_and_rest(sums):
    leading = sums.astype(jnp.bfloat16)
    return jnp.concatenate([leading, (sums - leading.astype(jnp.float32)).astype(jnp.bfloat16)], axis=0)


def hidden_kernel(core_ref, rows_ref, w_ref, send_ref, keep_ref):
    rows = rows_ref[...]
    wide = rows.astype(jnp.float32)
    sums = jnp.sum(wide * wide, axis=1, keepdims=True)
    lines = [
        jnp.sum(
            jnp.where(diagonal(), sums[c * CLASS_ROWS : (c + 1) * CLASS_ROWS], 0.0), axis=0, keepdims=True
        )
        for c in range(CLASSES)
    ]
    lines.append(jnp.zeros((SQUARES // 2 - CLASSES, UNIT), jnp.float32))
    squares = leading_and_rest(jnp.concatenate(lines, axis=0))

    columns = 2 * UNIT
    for k in range(4):
        out_ref = send_ref if k < 2 else keep_ref
        source = (k + 2 - 2 * core_ref[0]) % 4 * columns
        parts = jnp.dot(
            rows,
            w_ref[:, pl.ds(pl.multiple_of(source, columns), columns)],
            preferred_element_type=jnp.float32,
        )
        for half in range(2):
            piece = k % 2 * 2 + half
            out_ref[piece, :ROWS] = parts[:, half * UNIT : (half + 1) * UNIT].astype(jnp.bfloat16)
            out_ref[piece, ROWS:] = squares


def hidden_pieces(rows, w_in, core):
    units = w_in.shape[1]
    half = jax.ShapeDtypeStruct((units // (2 * UNIT), ROWS + SQUARES, UNIT), jnp.bfloat16)
    return pl.pallas_call(
        hidden_kernel,
        in_specs=[
            pl.BlockSpec(memory_space=pltpu.SMEM),
            pl.BlockSpec(memory_space=pltpu.VMEM),
            pl.BlockSpec(memory_space=pltpu.VMEM),
        ],
        out_shape=[half, half],
        compiler_params=pltpu.CompilerParams(vmem_limit_bytes=10 << 20),
        name="hidden_pieces",
    )(core.reshape(1), rows, w_in)


def core_kernel(own_ref, other_ref, out_ref):
    out_ref[:, :ROWS] = (
        own_ref[:, :ROWS].astype(jnp.float32) + other_ref[:, :ROWS].astype(jnp.float32)
    ).astype(jnp.bfloat16)
    both = own_ref[0, ROWS:].astype(jnp.float32) + other_ref[0, ROWS:].astype(jnp.float32)
    split = leading_and_rest(both[: SQUARES // 2] + both[SQUARES // 2 :])
    for piece in range(out_ref.shape[0]):
        out_ref[piece, ROWS:] = split


def core_summed(own, other):
    return pl.pallas_call(
        core_kernel,
        out_shape=jax.ShapeDtypeStruct(own.shape, jnp.bfloat16),
        compiler_params=pltpu.CompilerParams(vmem_limit_bytes=10 << 20),
        name="core_summed",
    )(own, other)


def silu_kernel(in_ref, out_ref):
    total = in_ref[0].astype(jnp.float32)
    for piece in range(1, in_ref.shape[0]):
        total = total + in_ref[piece].astype(jnp.float32)
    squares = total[ROWS : ROWS + SQUARES // 2] + total[ROWS + SQUARES // 2 :]
    for c in range(CLASSES):
        own = jnp.sum(jnp.where(diagonal(), squares[c : c + 1], 0.0), axis=1, keepdims=True)
        scaled = total[c * CLASS_ROWS : (c + 1) * CLASS_ROWS] * lax.rsqrt(own / D + NORM_EPSILON)
        hidden = (scaled / (1.0 + jnp.exp(-scaled))).astype(jnp.bfloat16)
        for piece in range(out_ref.shape[0]):
            out_ref[piece, c * CLASS_ROWS : (c + 1) * CLASS_ROWS] = hidden


def silu_copies(pieces):
    return pl.pallas_call(
        silu_kernel,
        out_shape=jax.ShapeDtypeStruct((pieces.shape[0], ROWS, UNIT), jnp.bfloat16),
        compiler_params=pltpu.CompilerParams(vmem_limit_bytes=10 << 20),
        name="silu_copies",
    )(pieces)


def compact_kernel(class_ref, received_ref, rows_ref, place_ref):
    width = rows_ref.shape[1]
    own_class = class_ref[0]
    received = received_ref[...].reshape(BLOCKS * PER_CLASS, width + META)
    slots = received.shape[0]
    row = lax.broadcasted_iota(jnp.int32, (slots, slots), 0)
    column = lax.broadcasted_iota(jnp.int32, (slots, slots), 1)
    earlier = (column // PER_CLASS < row // PER_CLASS) & (column % PER_CLASS == 0)
    earlier = earlier.astype(jnp.float32).astype(jnp.bfloat16)

    def earlier_sum(counts):
        return jnp.dot(earlier, counts, preferred_element_type=jnp.float32).astype(jnp.int32)

    counts = received[:, width:]
    named = counts.astype(jnp.float32).astype(jnp.int32)
    kept = jnp.clip(CAPACITY - earlier_sum(counts), 0, named)
    line = lax.broadcasted_iota(jnp.int32, named.shape, 0)
    block, place = line // PER_CLASS, line % PER_CLASS
    shift = (own_class + BLOCKS - block) % CLASSES
    in_class = (kept - shift + CLASSES - 1) // CLASSES
    first = earlier_sum(in_class.astype(jnp.float32).astype(jnp.bfloat16))
    spot = jnp.where(place < in_class, first + place, -1)
    chosen = spot == lax.broadcasted_iota(jnp.int32, named.shape, 1)
    chosen = chosen.astype(jnp.float32).astype(jnp.bfloat16)
    place_ref[...] = chosen
    rows = lax.dot_general(
        chosen, received[:, :width], (((0,), (0,)), ((), ())), preferred_element_type=jnp.float32
    )
    rows_ref[...] = rows[: rows_ref.shape[0]].astype(jnp.bfloat16)


def compacted(received, own_class):
    blocks, places, wide = received.shape
    return pl.pallas_call(
        compact_kernel,
        in_specs=[
            pl.BlockSpec(memory_space=pltpu.SMEM),
            pl.BlockSpec(memory_space=pltpu.VMEM),
        ],
        out_shape=[
            jax.ShapeDtypeStruct((CLASS_ROWS, wide - META), jnp.bfloat16),
            jax.ShapeDtypeStruct((blocks * places, META), jnp.bfloat16),
        ],
        compiler_params=pltpu.CompilerParams(vmem_limit_bytes=10 << 20),
        name="compacted",
    )(own_class.reshape(1), received)


def shards(
    residual, queries, keys, values, lengths, norm_gain, expert_ids, expert_weights, w_in, w_out
):
    tokens, width = residual.shape
    block = ((lax.axis_index("x") * 2 + lax.axis_index("zh")) * 2 + lax.axis_index("zq")) * 4 + lax.axis_index("zn")
    own_class = lax.axis_index("zn")

    summed, outgoing, mix_rows = tokens_packed(
        block, lengths, expert_ids, expert_weights, residual, queries, keys, values
    )
    gained = (w_in.astype(jnp.float32) * norm_gain.astype(jnp.float32)[:, None]).astype(jnp.bfloat16)
    received = lax.all_to_all(outgoing, DP, split_axis=0, concat_axis=0, tiled=True)
    class_rows, chosen = compacted(received, own_class)
    rows = lax.all_gather(class_rows, "zn", axis=0, tiled=True)
    send, own = hidden_pieces(rows, gained, lax.axis_index("core"))
    other = lax.ppermute(send, "core", ((0, 1), (1, 0)))
    pieces = lax.all_to_all(core_summed(own, other), "y", split_axis=0, concat_axis=0, tiled=True)
    gathered = lax.all_to_all(silu_copies(pieces), "y", split_axis=0, concat_axis=0, tiled=True)
    gathered = lax.all_gather(gathered, "core", axis=0, tiled=True)
    hidden = jnp.moveaxis(gathered, 0, 1).reshape(ROWS, 8 * UNIT)
    results = jnp.dot(hidden, w_out, preferred_element_type=jnp.float32).astype(jnp.bfloat16)

    class_out = summed_at_owner(results.reshape(CLASSES, CLASS_ROWS, width), "zn").astype(jnp.bfloat16)
    returned = jnp.dot(
        chosen[:, :CLASS_ROWS], class_out, preferred_element_type=jnp.float32
    ).astype(jnp.bfloat16)
    combined = lax.all_to_all(
        returned.reshape(BLOCKS, PER_CLASS, width), DP, split_axis=0, concat_axis=0, tiled=True
    )
    per_expert = jnp.sum(
        combined.reshape(EXPERTS, 2, SRC_CAP, width).astype(jnp.float32), axis=1
    ).reshape(EXPERTS * SRC_CAP, width)
    addition = jnp.einsum("st,sd->td", mix_rows, per_expert, precision=lax.Precision.HIGHEST)
    return (summed + addition).astype(jnp.bfloat16)


def solution(mesh):
    fine = Mesh(mesh.devices.reshape(4, 2, 2, 4, 4, 2), (*DP, *TENSOR))
    in_specs = (
        P(DP, TENSOR),
        P(DP, TENSOR),
        P(DP, None, TENSOR),
        P(DP, None, TENSOR),
        P(DP),
        P(TENSOR),
        P(DP, None),
        P(DP, None),
        P(TENSOR, DP),
        P(DP, TENSOR),
    )
    return jax.shard_map(shards, mesh=fine, in_specs=in_specs, out_specs=P(DP, TENSOR), check_vma=False)
```

```python
import jax
import jax.numpy as jnp
from jax import lax
from jax.experimental import pallas as pl
from jax.experimental.pallas import tpu as pltpu
from jax.sharding import Mesh, PartitionSpec as P

HEADS = 48
KV = 8
HEAD = 128
D = 6144
EXPERTS = 8
TOPK = 2
CACHE = 128
SRC_CAP = 16
BLOCKS = 64
CLASSES = 4
PER_CLASS = SRC_CAP // CLASSES
CAPACITY = 384
CLASS_ROWS = CAPACITY // CLASSES + BLOCKS * 6 // (4 * CLASSES)
META = 128
ROWS = CAPACITY
SLOT_ROWS = CAPACITY // CLASSES
SQUARES = 16
UNIT = 128
LINES = ROWS // UNIT

NORM_EPSILON = 1e-05

DP = ("x", "zh", "zq", "zn")
TENSOR = ("y", "core")


TOKENS = 32
STEP = 32
GROUP = HEADS // KV


def ranks(ids):
    experts = lax.broadcasted_iota(jnp.int32, (EXPERTS, TOKENS), 0)
    names = [(ids[k : k + 1] == experts).astype(jnp.float32) for k in range(TOPK)]
    named = names[0] + names[1]
    before = lax.broadcasted_iota(jnp.int32, (TOKENS, TOKENS), 0) < lax.broadcasted_iota(
        jnp.int32, (TOKENS, TOKENS), 1
    )
    earlier = jnp.dot(named, before.astype(jnp.float32), preferred_element_type=jnp.float32)
    rank = [jnp.sum(earlier * name, axis=0, keepdims=True).astype(jnp.int32) for name in names]
    return names, rank, named


def slot_iota():
    return lax.broadcasted_iota(jnp.int32, (EXPERTS * SRC_CAP, TOKENS), 0)


def packet_place(ids, rank, turn):
    return ids * SRC_CAP + (rank + turn) % CLASSES * PER_CLASS + rank // CLASSES


def tokens_kernel(
    block_ref, lengths_ref, ids_ref, residual_ref, queries_ref, keys_ref, values_ref,
    summed_ref, out_ref, query_ref, attended_ref, all_ref,
):
    step = pl.program_id(0)

    @pl.when(step == 0)
    def _():
        query_ref[...] = jnp.zeros_like(query_ref)

    for h in range(GROUP):
        query_ref[:, h, :] = queries_ref[:, h * HEAD : (h + 1) * HEAD].astype(jnp.float32)
    position = lax.broadcasted_iota(jnp.int32, (8, CACHE), 1)
    scores = []
    for t in range(STEP):
        products = lax.dot_general(
            query_ref[t].astype(jnp.bfloat16),
            keys_ref[t],
            (((1,), (1,)), ((), ())),
            preferred_element_type=jnp.float32,
        ) * HEAD ** (-0.5)
        scores.append(jnp.where(position < lengths_ref[step * STEP + t], products, -1e30))
    scores = jnp.concatenate(scores, axis=0)
    powered = jnp.exp(scores - jnp.max(scores, axis=1, keepdims=True))
    probs = powered / jnp.sum(powered, axis=1, keepdims=True)
    for t in range(STEP):
        attended_ref[t] = jnp.dot(
            probs[t * 8 : (t + 1) * 8].astype(jnp.bfloat16), values_ref[t], preferred_element_type=jnp.float32
        )
    for h in range(GROUP):
        lanes = slice(h * HEAD, (h + 1) * HEAD)
        total = residual_ref[:, lanes].astype(jnp.float32) + attended_ref[:, h, :]
        summed_ref[:, lanes] = total
        all_ref[pl.ds(pl.multiple_of(step * STEP, STEP), STEP), lanes] = total

    @pl.when(step == TOKENS // STEP - 1)
    def _():
        ids = ids_ref[...]
        _, rank, named = ranks(ids)
        pick = jnp.zeros((EXPERTS * SRC_CAP, TOKENS), jnp.float32)
        for k in range(TOPK):
            pick = jnp.where(slot_iota() == packet_place(ids[k : k + 1], rank[k], block_ref[0]), 1.0, pick)
        packed = jnp.dot(
            pick.astype(jnp.bfloat16), all_ref[...].astype(jnp.bfloat16), preferred_element_type=jnp.float32
        )
        width = packed.shape[1]
        own_lane = lax.broadcasted_iota(jnp.int32, (EXPERTS, META), 0) == lax.broadcasted_iota(
            jnp.int32, (EXPERTS, META), 1
        )
        counts = jnp.sum(named, axis=1, keepdims=True)
        counts = jnp.sum(jnp.where(own_lane, counts, 0.0), axis=0, keepdims=True)
        meta = jnp.broadcast_to(counts, (PER_CLASS, META)).astype(jnp.bfloat16)
        for e in range(EXPERTS):
            for c in range(CLASSES):
                first = e * SRC_CAP + c * PER_CLASS
                rows = packed[first : first + PER_CLASS].astype(jnp.bfloat16)
                for group in range(2):
                    peer = (e * 2 + group) * CLASSES + c
                    out_ref[peer, :, :width] = rows
                    out_ref[peer, :, width:] = meta


def tokens_packed(block, lengths, expert_ids, residual, queries, keys, values):
    tokens, width = residual.shape
    whole = lambda *shape: pl.BlockSpec(shape, lambda i: (0,) * len(shape))
    return pl.pallas_call(
        tokens_kernel,
        grid=(TOKENS // STEP,),
        in_specs=[
            pl.BlockSpec(memory_space=pltpu.SMEM),
            pl.BlockSpec(memory_space=pltpu.SMEM),
            whole(TOPK, TOKENS),
            pl.BlockSpec((STEP, width), lambda i: (i, 0)),
            pl.BlockSpec((STEP, width), lambda i: (i, 0)),
            pl.BlockSpec((STEP, CACHE, HEAD), lambda i: (i, 0, 0)),
            pl.BlockSpec((STEP, CACHE, HEAD), lambda i: (i, 0, 0)),
        ],
        out_specs=[
            pl.BlockSpec((STEP, width), lambda i: (i, 0)),
            whole(BLOCKS, PER_CLASS, width + META),
        ],
        out_shape=[
            jax.ShapeDtypeStruct((tokens, width), jnp.float32),
            jax.ShapeDtypeStruct((BLOCKS, PER_CLASS, width + META), jnp.bfloat16),
        ],
        scratch_shapes=[
            pltpu.VMEM((STEP, 8, HEAD), jnp.float32),
            pltpu.VMEM((STEP, 8, HEAD), jnp.float32),
            pltpu.VMEM((TOKENS, width), jnp.float32),
        ],
        compiler_params=pltpu.CompilerParams(vmem_limit_bytes=10 << 20),
        name="tokens_packed",
    )(
        block.reshape(1),
        *(
            pltpu.with_memory_space_constraint(operand, pltpu.HBM)
            for operand in (lengths, expert_ids.T, residual, queries, keys, values)
        ),
    )


def summed_at_owner(pieces, axis):
    return jnp.sum(
        lax.all_to_all(pieces, axis, split_axis=0, concat_axis=0, tiled=True).astype(jnp.float32), axis=0
    )


def diagonal():
    row = lax.broadcasted_iota(jnp.int32, (UNIT, UNIT), 0)
    return row == lax.broadcasted_iota(jnp.int32, (UNIT, UNIT), 1)


def leading_and_rest(sums):
    leading = sums.astype(jnp.bfloat16)
    return jnp.concatenate([leading, (sums - leading.astype(jnp.float32)).astype(jnp.bfloat16)], axis=0)


def hidden_kernel(core_ref, place_ref, gathered_ref, w_ref, send_ref, keep_ref):
    wide = lax.dot_general(
        place_ref[...], gathered_ref[...], (((0,), (0,)), ((), ())), preferred_element_type=jnp.float32
    )
    rows = wide.astype(jnp.bfloat16)
    sums = jnp.sum(wide * wide, axis=1, keepdims=True)
    lines = [
        jnp.sum(jnp.where(diagonal(), sums[g * UNIT : (g + 1) * UNIT], 0.0), axis=0, keepdims=True)
        for g in range(LINES)
    ]
    lines.append(jnp.zeros((SQUARES // 2 - LINES, UNIT), jnp.float32))
    squares = leading_and_rest(jnp.concatenate(lines, axis=0))

    columns = 2 * UNIT
    for k in range(4):
        out_ref = send_ref if k < 2 else keep_ref
        source = (k + 2 - 2 * core_ref[0]) % 4 * columns
        parts = jnp.dot(
            rows,
            w_ref[:, pl.ds(pl.multiple_of(source, columns), columns)],
            preferred_element_type=jnp.float32,
        )
        for half in range(2):
            piece = k % 2 * 2 + half
            out_ref[piece, :ROWS] = parts[:, half * UNIT : (half + 1) * UNIT].astype(jnp.bfloat16)
            out_ref[piece, ROWS:] = squares


def hidden_pieces(place, gathered, w_in, core):
    units = w_in.shape[1]
    half = jax.ShapeDtypeStruct((units // (2 * UNIT), ROWS + SQUARES, UNIT), jnp.bfloat16)
    return pl.pallas_call(
        hidden_kernel,
        in_specs=[
            pl.BlockSpec(memory_space=pltpu.SMEM),
            pl.BlockSpec(memory_space=pltpu.VMEM),
            pl.BlockSpec(memory_space=pltpu.VMEM),
            pl.BlockSpec(memory_space=pltpu.VMEM),
        ],
        out_shape=[half, half],
        compiler_params=pltpu.CompilerParams(vmem_limit_bytes=10 << 20),
        name="hidden_pieces",
    )(core.reshape(1), place, gathered, w_in)


def core_kernel(own_ref, other_ref, out_ref):
    out_ref[:, :ROWS] = (
        own_ref[:, :ROWS].astype(jnp.float32) + other_ref[:, :ROWS].astype(jnp.float32)
    ).astype(jnp.bfloat16)
    both = own_ref[0, ROWS:].astype(jnp.float32) + other_ref[0, ROWS:].astype(jnp.float32)
    split = leading_and_rest(both[: SQUARES // 2] + both[SQUARES // 2 :])
    for piece in range(out_ref.shape[0]):
        out_ref[piece, ROWS:] = split


def core_summed(own, other):
    return pl.pallas_call(
        core_kernel,
        out_shape=jax.ShapeDtypeStruct(own.shape, jnp.bfloat16),
        compiler_params=pltpu.CompilerParams(vmem_limit_bytes=10 << 20),
        name="core_summed",
    )(own, other)


def silu_kernel(in_ref, out_ref):
    total = in_ref[0].astype(jnp.float32)
    for piece in range(1, in_ref.shape[0]):
        total = total + in_ref[piece].astype(jnp.float32)
    squares = total[ROWS : ROWS + SQUARES // 2] + total[ROWS + SQUARES // 2 :]
    for g in range(LINES):
        own = jnp.sum(jnp.where(diagonal(), squares[g : g + 1], 0.0), axis=1, keepdims=True)
        scaled = total[g * UNIT : (g + 1) * UNIT] * lax.rsqrt(own / D + NORM_EPSILON)
        hidden = (scaled / (1.0 + jnp.exp(-scaled))).astype(jnp.bfloat16)
        for piece in range(out_ref.shape[0]):
            out_ref[piece, g * UNIT : (g + 1) * UNIT] = hidden


def silu_copies(pieces):
    return pl.pallas_call(
        silu_kernel,
        out_shape=jax.ShapeDtypeStruct((pieces.shape[0], ROWS, UNIT), jnp.bfloat16),
        compiler_params=pltpu.CompilerParams(vmem_limit_bytes=10 << 20),
        name="silu_copies",
    )(pieces)


def output_kernel(hidden_ref, w_ref, out_ref):
    hidden = jnp.concatenate([hidden_ref[piece] for piece in range(hidden_ref.shape[0])], axis=1)
    out_ref[...] = jnp.dot(hidden, w_ref[...], preferred_element_type=jnp.float32).astype(jnp.bfloat16)


def output_parts(hidden, w_out):
    return pl.pallas_call(
        output_kernel,
        in_specs=[pl.BlockSpec(memory_space=pltpu.VMEM)] * 2,
        out_shape=jax.ShapeDtypeStruct((ROWS, w_out.shape[1]), jnp.bfloat16),
        compiler_params=pltpu.CompilerParams(vmem_limit_bytes=10 << 20),
        name="output_parts",
    )(hidden, w_out)


def flags(condition):
    return condition.astype(jnp.float32).astype(jnp.bfloat16)


def compact_kernel(here_ref, ids_ref, weights_ref, received_ref, rows_ref, place_ref, back_ref, mix_ref):
    width = rows_ref.shape[1]
    own_block, own_class = here_ref[0], here_ref[1]
    received = received_ref[...].reshape(BLOCKS * PER_CLASS, width + META)
    slots = received.shape[0]
    row = lax.broadcasted_iota(jnp.int32, (slots, slots), 0)
    column = lax.broadcasted_iota(jnp.int32, (slots, slots), 1)
    earlier = flags((column // PER_CLASS < row // PER_CLASS) & (column % PER_CLASS == 0))

    def earlier_sum(counts):
        return jnp.dot(earlier, counts, preferred_element_type=jnp.float32).astype(jnp.int32)

    all_counts = received[:, width:]
    own_expert = own_block // (BLOCKS // EXPERTS)
    counts = jnp.dot(
        all_counts,
        flags(lax.broadcasted_iota(jnp.int32, (META, META), 0) == own_expert),
        preferred_element_type=jnp.float32,
    )
    named = counts.astype(jnp.int32)
    offset = earlier_sum(counts.astype(jnp.bfloat16))
    kept = jnp.clip(CAPACITY - offset, 0, named)
    line = lax.broadcasted_iota(jnp.int32, named.shape, 0)
    lane = lax.broadcasted_iota(jnp.int32, named.shape, 1)
    block, place = line // PER_CLASS, line % PER_CLASS

    def class_order(of_class):
        shift = (of_class + BLOCKS - block) % CLASSES
        in_class = (kept - shift + CLASSES - 1) // CLASSES
        first = earlier_sum(in_class.astype(jnp.float32).astype(jnp.bfloat16))
        live = place < in_class
        slot = jnp.where(live, offset + place * CLASSES + shift + 1, 0)
        return flags((first + place == lane) & live), slot

    chosen, _ = class_order(own_class)
    rows = lax.dot_general(
        chosen, received[:, :width], (((0,), (0,)), ((), ())), preferred_element_type=jnp.float32
    )
    rows_ref[...] = rows[:CLASS_ROWS].astype(jnp.bfloat16)

    for c in range(CLASSES):
        chosen, slot = class_order(c)
        digits = jnp.where(lane < META // 2, slot // 16, slot % 16).astype(jnp.float32).astype(jnp.bfloat16)
        found = lax.dot_general(chosen, digits, (((0,), (0,)), ((), ())), preferred_element_type=jnp.float32)
        found = found[:CLASS_ROWS, :1] * 16.0 + found[:CLASS_ROWS, META // 2 : META // 2 + 1]
        found = found.astype(jnp.int32) - 1
        target = jnp.where(found < 0, -1, found % CLASSES * SLOT_ROWS + found // CLASSES)
        place_ref[c * CLASS_ROWS : (c + 1) * CLASS_ROWS] = flags(
            target == lax.broadcasted_iota(jnp.int32, (CLASS_ROWS, ROWS), 1)
        )

    rank = place * CLASSES + (own_class + CLASSES * BLOCKS * SRC_CAP - offset) % CLASSES
    back_ref[...] = flags(((offset + rank - own_class) // CLASSES == lane) & (rank < kept))

    ids = ids_ref[...]
    names, rank, _ = ranks(ids)
    offsets = lax.dot_general(
        all_counts,
        flags((block < own_block) & (place == 0)),
        (((0,), (0,)), ((), ())),
        preferred_element_type=jnp.float32,
    )[:EXPERTS, :TOKENS]
    mix = jnp.zeros(mix_ref.shape, jnp.float32)
    for k in range(TOPK):
        turn = jnp.sum(offsets * names[k], axis=0, keepdims=True).astype(jnp.int32)
        mix = jnp.where(
            slot_iota() == packet_place(ids[k : k + 1], rank[k], turn), weights_ref[k : k + 1], mix
        )
    mix_ref[...] = mix


def compacted(received, own_block, own_class, expert_ids, expert_weights):
    blocks, places, wide = received.shape
    return pl.pallas_call(
        compact_kernel,
        in_specs=[
            pl.BlockSpec(memory_space=pltpu.SMEM),
            pl.BlockSpec(memory_space=pltpu.VMEM),
            pl.BlockSpec(memory_space=pltpu.VMEM),
            pl.BlockSpec(memory_space=pltpu.VMEM),
        ],
        out_shape=[
            jax.ShapeDtypeStruct((CLASS_ROWS, wide - META), jnp.bfloat16),
            jax.ShapeDtypeStruct((CLASSES * CLASS_ROWS, ROWS), jnp.bfloat16),
            jax.ShapeDtypeStruct((blocks * places, META), jnp.bfloat16),
            jax.ShapeDtypeStruct((EXPERTS * SRC_CAP, TOKENS), jnp.float32),
        ],
        compiler_params=pltpu.CompilerParams(vmem_limit_bytes=10 << 20),
        name="compacted",
    )(jnp.stack([own_block, own_class]), expert_ids.T, expert_weights.T, received)


def shards(
    residual, queries, keys, values, lengths, norm_gain, expert_ids, expert_weights, w_in, w_out
):
    tokens, width = residual.shape
    block = ((lax.axis_index("x") * 2 + lax.axis_index("zh")) * 2 + lax.axis_index("zq")) * 4 + lax.axis_index("zn")
    own_class = lax.axis_index("zn")

    summed, outgoing = tokens_packed(block, lengths, expert_ids, residual, queries, keys, values)
    gained = (w_in.astype(jnp.float32) * norm_gain.astype(jnp.float32)[:, None]).astype(jnp.bfloat16)
    received = lax.all_to_all(outgoing, DP, split_axis=0, concat_axis=0, tiled=True)
    class_rows, place, back, mix_rows = compacted(received, block, own_class, expert_ids, expert_weights)
    rows = lax.all_gather(class_rows, "zn", axis=0, tiled=True)
    send, own = hidden_pieces(place, rows, gained, lax.axis_index("core"))
    other = lax.ppermute(send, "core", ((0, 1), (1, 0)))
    pieces = lax.all_to_all(core_summed(own, other), "y", split_axis=0, concat_axis=0, tiled=True)
    gathered = lax.all_to_all(silu_copies(pieces), "y", split_axis=0, concat_axis=0, tiled=True)
    gathered = lax.all_gather(gathered, "core", axis=0, tiled=True)
    results = output_parts(gathered, w_out)

    class_out = summed_at_owner(results.reshape(CLASSES, SLOT_ROWS, width), "zn").astype(jnp.bfloat16)
    returned = jnp.dot(
        back[:, :SLOT_ROWS], class_out, preferred_element_type=jnp.float32
    ).astype(jnp.bfloat16)
    combined = lax.all_to_all(
        returned.reshape(BLOCKS, PER_CLASS, width), DP, split_axis=0, concat_axis=0, tiled=True
    )
    per_expert = jnp.sum(
        combined.reshape(EXPERTS, 2, SRC_CAP, width).astype(jnp.float32), axis=1
    ).reshape(EXPERTS * SRC_CAP, width)
    addition = jnp.einsum("st,sd->td", mix_rows, per_expert, precision=lax.Precision.HIGHEST)
    return (summed + addition).astype(jnp.bfloat16)


def solution(mesh):
    fine = Mesh(mesh.devices.reshape(4, 2, 2, 4, 4, 2), (*DP, *TENSOR))
    in_specs = (
        P(DP, TENSOR),
        P(DP, TENSOR),
        P(DP, None, TENSOR),
        P(DP, None, TENSOR),
        P(DP),
        P(TENSOR),
        P(DP, None),
        P(DP, None),
        P(TENSOR, DP),
        P(DP, TENSOR),
    )
    return jax.shard_map(shards, mesh=fine, in_specs=in_specs, out_specs=P(DP, TENSOR), check_vma=False)
```

```python
import jax
import jax.numpy as jnp
from jax import lax
from jax.experimental import pallas as pl
from jax.experimental.pallas import tpu as pltpu
from jax.sharding import Mesh, PartitionSpec as P

HEADS = 48
KV = 8
HEAD = 128
D = 6144
EXPERTS = 8
TOPK = 2
CACHE = 128
SRC_CAP = 16
BLOCKS = 64
CLASSES = 4
PER_CLASS = SRC_CAP // CLASSES
CAPACITY = 384
CLASS_ROWS = CAPACITY // CLASSES + BLOCKS * 6 // (4 * CLASSES)
META = 128
ROWS = CAPACITY
SLOT_ROWS = CAPACITY // CLASSES
SQUARES = 16
UNIT = 128
LINES = ROWS // UNIT

NORM_EPSILON = 1e-05

DP = ("x", "zh", "zq", "zn")
TENSOR = ("y", "core")


TOKENS = 32
STEP = 32
GROUP = HEADS // KV


def ranks(ids):
    experts = lax.broadcasted_iota(jnp.int32, (EXPERTS, TOKENS), 0)
    names = [(ids[k : k + 1] == experts).astype(jnp.float32) for k in range(TOPK)]
    named = names[0] + names[1]
    before = lax.broadcasted_iota(jnp.int32, (TOKENS, TOKENS), 0) < lax.broadcasted_iota(
        jnp.int32, (TOKENS, TOKENS), 1
    )
    earlier = jnp.dot(named, before.astype(jnp.float32), preferred_element_type=jnp.float32)
    rank = [jnp.sum(earlier * name, axis=0, keepdims=True).astype(jnp.int32) for name in names]
    return names, rank, named


def slot_iota():
    return lax.broadcasted_iota(jnp.int32, (EXPERTS * SRC_CAP, TOKENS), 0)


def packet_place(ids, rank, turn):
    return ids * SRC_CAP + (rank + turn) % CLASSES * PER_CLASS + rank // CLASSES


def tokens_kernel(
    block_ref, lengths_ref, ids_ref, residual_ref, queries_ref, keys_ref, values_ref,
    summed_ref, out_ref, query_ref, attended_ref, all_ref,
):
    step = pl.program_id(0)

    @pl.when(step == 0)
    def _():
        query_ref[...] = jnp.zeros_like(query_ref)

    for h in range(GROUP):
        query_ref[:, h, :] = queries_ref[:, h * HEAD : (h + 1) * HEAD].astype(jnp.float32)
    position = lax.broadcasted_iota(jnp.int32, (8, CACHE), 1)
    scores = []
    for t in range(STEP):
        products = lax.dot_general(
            query_ref[t].astype(jnp.bfloat16),
            keys_ref[t],
            (((1,), (1,)), ((), ())),
            preferred_element_type=jnp.float32,
        ) * HEAD ** (-0.5)
        scores.append(jnp.where(position < lengths_ref[step * STEP + t], products, -1e30))
    scores = jnp.concatenate(scores, axis=0)
    powered = jnp.exp(scores - jnp.max(scores, axis=1, keepdims=True))
    probs = powered / jnp.sum(powered, axis=1, keepdims=True)
    for t in range(STEP):
        attended_ref[t] = jnp.dot(
            probs[t * 8 : (t + 1) * 8].astype(jnp.bfloat16), values_ref[t], preferred_element_type=jnp.float32
        )
    for h in range(GROUP):
        lanes = slice(h * HEAD, (h + 1) * HEAD)
        total = residual_ref[:, lanes].astype(jnp.float32) + attended_ref[:, h, :]
        summed_ref[:, lanes] = total
        all_ref[pl.ds(pl.multiple_of(step * STEP, STEP), STEP), lanes] = total

    @pl.when(step == TOKENS // STEP - 1)
    def _():
        ids = ids_ref[...]
        _, rank, named = ranks(ids)
        pick = jnp.zeros((EXPERTS * SRC_CAP, TOKENS), jnp.float32)
        for k in range(TOPK):
            pick = jnp.where(slot_iota() == packet_place(ids[k : k + 1], rank[k], block_ref[0]), 1.0, pick)
        packed = jnp.dot(
            pick.astype(jnp.bfloat16), all_ref[...].astype(jnp.bfloat16), preferred_element_type=jnp.float32
        )
        width = packed.shape[1]
        own_lane = lax.broadcasted_iota(jnp.int32, (EXPERTS, META), 0) == lax.broadcasted_iota(
            jnp.int32, (EXPERTS, META), 1
        )
        counts = jnp.sum(named, axis=1, keepdims=True)
        counts = jnp.sum(jnp.where(own_lane, counts, 0.0), axis=0, keepdims=True)
        meta = jnp.broadcast_to(counts, (PER_CLASS, META)).astype(jnp.bfloat16)
        for e in range(EXPERTS):
            for c in range(CLASSES):
                first = e * SRC_CAP + c * PER_CLASS
                rows = packed[first : first + PER_CLASS].astype(jnp.bfloat16)
                for group in range(2):
                    peer = (e * 2 + group) * CLASSES + c
                    out_ref[peer, :, :width] = rows
                    out_ref[peer, :, width:] = meta


def tokens_packed(block, lengths, expert_ids, residual, queries, keys, values):
    tokens, width = residual.shape
    whole = lambda *shape: pl.BlockSpec(shape, lambda i: (0,) * len(shape))
    return pl.pallas_call(
        tokens_kernel,
        grid=(TOKENS // STEP,),
        in_specs=[
            pl.BlockSpec(memory_space=pltpu.SMEM),
            pl.BlockSpec(memory_space=pltpu.SMEM),
            whole(TOPK, TOKENS),
            pl.BlockSpec((STEP, width), lambda i: (i, 0)),
            pl.BlockSpec((STEP, width), lambda i: (i, 0)),
            pl.BlockSpec((STEP, CACHE, HEAD), lambda i: (i, 0, 0)),
            pl.BlockSpec((STEP, CACHE, HEAD), lambda i: (i, 0, 0)),
        ],
        out_specs=[
            pl.BlockSpec((STEP, width), lambda i: (i, 0)),
            whole(BLOCKS, PER_CLASS, width + META),
        ],
        out_shape=[
            jax.ShapeDtypeStruct((tokens, width), jnp.float32),
            jax.ShapeDtypeStruct((BLOCKS, PER_CLASS, width + META), jnp.bfloat16),
        ],
        scratch_shapes=[
            pltpu.VMEM((STEP, 8, HEAD), jnp.float32),
            pltpu.VMEM((STEP, 8, HEAD), jnp.float32),
            pltpu.VMEM((TOKENS, width), jnp.float32),
        ],
        compiler_params=pltpu.CompilerParams(vmem_limit_bytes=10 << 20),
        name="tokens_packed",
    )(
        block.reshape(1),
        *(
            pltpu.with_memory_space_constraint(operand, pltpu.HBM)
            for operand in (lengths, expert_ids.T, residual, queries, keys, values)
        ),
    )


def summed_at_owner(pieces, axis):
    return jnp.sum(
        lax.all_to_all(pieces, axis, split_axis=0, concat_axis=0, tiled=True).astype(jnp.float32), axis=0
    )


def diagonal():
    row = lax.broadcasted_iota(jnp.int32, (UNIT, UNIT), 0)
    return row == lax.broadcasted_iota(jnp.int32, (UNIT, UNIT), 1)


def leading_and_rest(sums):
    leading = sums.astype(jnp.bfloat16)
    return jnp.concatenate([leading, (sums - leading.astype(jnp.float32)).astype(jnp.bfloat16)], axis=0)


def write_pieces(rows, squares, w_ref, half, out_ref):
    columns = 2 * UNIT
    for k in range(2):
        source = (half * 2 + k) * columns
        parts = jnp.dot(
            rows,
            w_ref[:, pl.ds(pl.multiple_of(source, columns), columns)],
            preferred_element_type=jnp.float32,
        )
        for side in range(2):
            piece = k * 2 + side
            out_ref[piece, :ROWS] = parts[:, side * UNIT : (side + 1) * UNIT].astype(jnp.bfloat16)
            out_ref[piece, ROWS:] = squares


def sent_kernel(core_ref, place_ref, gathered_ref, w_ref, send_ref, rows_ref, squares_ref):
    wide = lax.dot_general(
        place_ref[...], gathered_ref[...], (((0,), (0,)), ((), ())), preferred_element_type=jnp.float32
    )
    rows = wide.astype(jnp.bfloat16)
    rows_ref[...] = rows
    sums = jnp.sum(wide * wide, axis=1, keepdims=True)
    lines = [
        jnp.sum(jnp.where(diagonal(), sums[g * UNIT : (g + 1) * UNIT], 0.0), axis=0, keepdims=True)
        for g in range(LINES)
    ]
    lines.append(jnp.zeros((SQUARES // 2 - LINES, UNIT), jnp.float32))
    squares = leading_and_rest(jnp.concatenate(lines, axis=0))
    squares_ref[...] = squares
    write_pieces(rows, squares, w_ref, 1 - core_ref[0], send_ref)


def kept_kernel(core_ref, rows_ref, squares_ref, w_ref, keep_ref):
    write_pieces(rows_ref[...], squares_ref[...], w_ref, core_ref[0], keep_ref)


def first_product(kernel, name, out_shape, core, *operands):
    return pl.pallas_call(
        kernel,
        in_specs=[
            pl.BlockSpec(memory_space=pltpu.SMEM),
            *[pl.BlockSpec(memory_space=pltpu.VMEM)] * len(operands),
        ],
        out_shape=out_shape,
        compiler_params=pltpu.CompilerParams(vmem_limit_bytes=10 << 20),
        name=name,
    )(core.reshape(1), *operands)


def half_of_units(w_in):
    return jax.ShapeDtypeStruct((w_in.shape[1] // (2 * UNIT), ROWS + SQUARES, UNIT), jnp.bfloat16)


def sent_pieces(place, gathered, w_in, core):
    out_shape = [
        half_of_units(w_in),
        jax.ShapeDtypeStruct((ROWS, gathered.shape[1]), jnp.bfloat16),
        jax.ShapeDtypeStruct((SQUARES, UNIT), jnp.bfloat16),
    ]
    return first_product(sent_kernel, "sent_pieces", out_shape, core, place, gathered, w_in)


def kept_pieces(rows, squares, w_in, core):
    return first_product(kept_kernel, "kept_pieces", half_of_units(w_in), core, rows, squares, w_in)


def core_kernel(own_ref, other_ref, out_ref):
    out_ref[:, :ROWS] = (
        own_ref[:, :ROWS].astype(jnp.float32) + other_ref[:, :ROWS].astype(jnp.float32)
    ).astype(jnp.bfloat16)
    both = own_ref[0, ROWS:].astype(jnp.float32) + other_ref[0, ROWS:].astype(jnp.float32)
    split = leading_and_rest(both[: SQUARES // 2] + both[SQUARES // 2 :])
    for piece in range(out_ref.shape[0]):
        out_ref[piece, ROWS:] = split


def core_summed(own, other):
    return pl.pallas_call(
        core_kernel,
        out_shape=jax.ShapeDtypeStruct(own.shape, jnp.bfloat16),
        compiler_params=pltpu.CompilerParams(vmem_limit_bytes=10 << 20),
        name="core_summed",
    )(own, other)


def silu_kernel(in_ref, out_ref):
    total = in_ref[0].astype(jnp.float32)
    for piece in range(1, in_ref.shape[0]):
        total = total + in_ref[piece].astype(jnp.float32)
    squares = total[ROWS : ROWS + SQUARES // 2] + total[ROWS + SQUARES // 2 :]
    for g in range(LINES):
        own = jnp.sum(jnp.where(diagonal(), squares[g : g + 1], 0.0), axis=1, keepdims=True)
        scaled = total[g * UNIT : (g + 1) * UNIT] * lax.rsqrt(own / D + NORM_EPSILON)
        hidden = (scaled / (1.0 + jnp.exp(-scaled))).astype(jnp.bfloat16)
        for piece in range(out_ref.shape[0]):
            out_ref[piece, g * UNIT : (g + 1) * UNIT] = hidden


def silu_copies(pieces):
    return pl.pallas_call(
        silu_kernel,
        out_shape=jax.ShapeDtypeStruct((pieces.shape[0], ROWS, UNIT), jnp.bfloat16),
        compiler_params=pltpu.CompilerParams(vmem_limit_bytes=10 << 20),
        name="silu_copies",
    )(pieces)


def output_kernel(hidden_ref, w_ref, out_ref):
    hidden = jnp.concatenate([hidden_ref[piece] for piece in range(hidden_ref.shape[0])], axis=1)
    out_ref[...] = jnp.dot(hidden, w_ref[...], preferred_element_type=jnp.float32).astype(jnp.bfloat16)


def output_parts(hidden, w_out):
    return pl.pallas_call(
        output_kernel,
        in_specs=[pl.BlockSpec(memory_space=pltpu.VMEM)] * 2,
        out_shape=jax.ShapeDtypeStruct((ROWS, w_out.shape[1]), jnp.bfloat16),
        compiler_params=pltpu.CompilerParams(vmem_limit_bytes=10 << 20),
        name="output_parts",
    )(hidden, w_out)


def flags(condition):
    return condition.astype(jnp.float32).astype(jnp.bfloat16)


def kept_of_blocks(all_counts, own_block):
    slots = all_counts.shape[0]
    row = lax.broadcasted_iota(jnp.int32, (slots, slots), 0)
    column = lax.broadcasted_iota(jnp.int32, (slots, slots), 1)
    earlier = flags((column // PER_CLASS < row // PER_CLASS) & (column % PER_CLASS == 0))

    def earlier_sum(counts):
        return jnp.dot(earlier, counts, preferred_element_type=jnp.float32).astype(jnp.int32)

    own_expert = own_block // (BLOCKS // EXPERTS)
    counts = jnp.dot(
        all_counts,
        flags(lax.broadcasted_iota(jnp.int32, (META, META), 0) == own_expert),
        preferred_element_type=jnp.float32,
    )
    offset = earlier_sum(counts.astype(jnp.bfloat16))
    return offset, jnp.clip(CAPACITY - offset, 0, counts.astype(jnp.int32)), earlier_sum


def compact_kernel(here_ref, received_ref, rows_ref, place_ref, counts_ref):
    width = rows_ref.shape[1]
    received = received_ref[...].reshape(BLOCKS * PER_CLASS, width + META)
    all_counts = received[:, width:]
    counts_ref[...] = all_counts
    offset, kept, earlier_sum = kept_of_blocks(all_counts, here_ref[0])
    line = lax.broadcasted_iota(jnp.int32, kept.shape, 0)
    lane = lax.broadcasted_iota(jnp.int32, kept.shape, 1)
    block, place = line // PER_CLASS, line % PER_CLASS

    def class_order(of_class):
        shift = (of_class + BLOCKS - block) % CLASSES
        in_class = (kept - shift + CLASSES - 1) // CLASSES
        first = earlier_sum(in_class.astype(jnp.float32).astype(jnp.bfloat16))
        live = place < in_class
        slot = jnp.where(live, offset + place * CLASSES + shift + 1, 0)
        return flags((first + place == lane) & live), slot

    chosen, _ = class_order(here_ref[1])
    rows = lax.dot_general(
        chosen, received[:, :width], (((0,), (0,)), ((), ())), preferred_element_type=jnp.float32
    )
    rows_ref[...] = rows[:CLASS_ROWS].astype(jnp.bfloat16)

    for c in range(CLASSES):
        chosen, slot = class_order(c)
        digits = jnp.where(lane < META // 2, slot // 16, slot % 16).astype(jnp.float32).astype(jnp.bfloat16)
        found = lax.dot_general(chosen, digits, (((0,), (0,)), ((), ())), preferred_element_type=jnp.float32)
        found = found[:CLASS_ROWS, :1] * 16.0 + found[:CLASS_ROWS, META // 2 : META // 2 + 1]
        found = found.astype(jnp.int32) - 1
        target = jnp.where(found < 0, -1, found % CLASSES * SLOT_ROWS + found // CLASSES)
        place_ref[c * CLASS_ROWS : (c + 1) * CLASS_ROWS] = flags(
            target == lax.broadcasted_iota(jnp.int32, (CLASS_ROWS, ROWS), 1)
        )


def compacted(received, own_block, own_class):
    blocks, places, wide = received.shape
    return pl.pallas_call(
        compact_kernel,
        in_specs=[
            pl.BlockSpec(memory_space=pltpu.SMEM),
            pl.BlockSpec(memory_space=pltpu.VMEM),
        ],
        out_shape=[
            jax.ShapeDtypeStruct((CLASS_ROWS, wide - META), jnp.bfloat16),
            jax.ShapeDtypeStruct((CLASSES * CLASS_ROWS, ROWS), jnp.bfloat16),
            jax.ShapeDtypeStruct((blocks * places, META), jnp.bfloat16),
        ],
        compiler_params=pltpu.CompilerParams(vmem_limit_bytes=10 << 20),
        name="compacted",
    )(jnp.stack([own_block, own_class]), received)


def back_kernel(here_ref, ids_ref, weights_ref, counts_ref, back_ref, mix_ref):
    own_block, own_class = here_ref[0], here_ref[1]
    all_counts = counts_ref[...]
    offset, kept, _ = kept_of_blocks(all_counts, own_block)
    line = lax.broadcasted_iota(jnp.int32, kept.shape, 0)
    lane = lax.broadcasted_iota(jnp.int32, kept.shape, 1)
    block, place = line // PER_CLASS, line % PER_CLASS
    rank = place * CLASSES + (own_class + CLASSES * BLOCKS * SRC_CAP - offset) % CLASSES
    back_ref[...] = flags(((offset + rank - own_class) // CLASSES == lane) & (rank < kept))

    ids = ids_ref[...]
    names, rank, _ = ranks(ids)
    offsets = lax.dot_general(
        all_counts,
        flags((block < own_block) & (place == 0)),
        (((0,), (0,)), ((), ())),
        preferred_element_type=jnp.float32,
    )[:EXPERTS, :TOKENS]
    mix = jnp.zeros((EXPERTS * SRC_CAP, TOKENS), jnp.float32)
    for k in range(TOPK):
        turn = jnp.sum(offsets * names[k], axis=0, keepdims=True).astype(jnp.int32)
        mix = jnp.where(
            slot_iota() == packet_place(ids[k : k + 1], rank[k], turn), weights_ref[k : k + 1], mix
        )
    for part in range(3):
        rounded = mix.astype(jnp.bfloat16)
        for e in range(EXPERTS):
            for group in range(2):
                first = (e * 2 + group) * SRC_CAP
                mix_ref[part, first : first + SRC_CAP] = rounded[e * SRC_CAP : (e + 1) * SRC_CAP]
        mix = mix - rounded.astype(jnp.float32)


def way_back(counts, own_block, own_class, expert_ids, expert_weights):
    return pl.pallas_call(
        back_kernel,
        in_specs=[
            pl.BlockSpec(memory_space=pltpu.SMEM),
            pl.BlockSpec(memory_space=pltpu.VMEM),
            pl.BlockSpec(memory_space=pltpu.VMEM),
            pl.BlockSpec(memory_space=pltpu.VMEM),
        ],
        out_shape=[
            jax.ShapeDtypeStruct(counts.shape, jnp.bfloat16),
            jax.ShapeDtypeStruct((3, 2 * EXPERTS * SRC_CAP, TOKENS), jnp.bfloat16),
        ],
        compiler_params=pltpu.CompilerParams(vmem_limit_bytes=10 << 20),
        name="way_back",
    )(jnp.stack([own_block, own_class]), expert_ids.T, expert_weights.T, counts)


def final_kernel(summed_ref, combined_ref, mix_ref, out_ref):
    total = summed_ref[...]
    rows = combined_ref[...].reshape(BLOCKS * PER_CLASS, total.shape[1])
    for part in (2, 1, 0):
        total = total + lax.dot_general(
            mix_ref[part], rows, (((0,), (0,)), ((), ())), preferred_element_type=jnp.float32
        )
    out_ref[...] = total.astype(jnp.bfloat16)


def final_rows(summed, combined, mix):
    return pl.pallas_call(
        final_kernel,
        in_specs=[pl.BlockSpec(memory_space=pltpu.VMEM)] * 3,
        out_shape=jax.ShapeDtypeStruct(summed.shape, jnp.bfloat16),
        compiler_params=pltpu.CompilerParams(vmem_limit_bytes=10 << 20),
        name="final_rows",
    )(summed, combined, mix)


def shards(
    residual, queries, keys, values, lengths, norm_gain, expert_ids, expert_weights, w_in, w_out
):
    tokens, width = residual.shape
    block = ((lax.axis_index("x") * 2 + lax.axis_index("zh")) * 2 + lax.axis_index("zq")) * 4 + lax.axis_index("zn")
    own_class = lax.axis_index("zn")

    summed, outgoing = tokens_packed(block, lengths, expert_ids, residual, queries, keys, values)
    gained = (w_in.astype(jnp.float32) * norm_gain.astype(jnp.float32)[:, None]).astype(jnp.bfloat16)
    received = lax.all_to_all(outgoing, DP, split_axis=0, concat_axis=0, tiled=True)
    class_rows, place, counts = compacted(received, block, own_class)
    rows = lax.all_gather(class_rows, "zn", axis=0, tiled=True)
    core = lax.axis_index("core")
    send, rows, squares = sent_pieces(place, rows, gained, core)
    other = lax.ppermute(send, "core", ((0, 1), (1, 0)))
    own = kept_pieces(rows, squares, gained, core)
    counts, squares = lax.optimization_barrier((counts, squares))
    back, mix = way_back(counts, block, own_class, expert_ids, expert_weights)
    own, back, mix = lax.optimization_barrier((own, back, mix))
    pieces = lax.all_to_all(core_summed(own, other), "y", split_axis=0, concat_axis=0, tiled=True)
    gathered = lax.all_to_all(silu_copies(pieces), "y", split_axis=0, concat_axis=0, tiled=True)
    gathered = lax.all_gather(gathered, "core", axis=0, tiled=True)
    results = output_parts(gathered, w_out)

    class_out = summed_at_owner(results.reshape(CLASSES, SLOT_ROWS, width), "zn").astype(jnp.bfloat16)
    returned = jnp.dot(
        back[:, :SLOT_ROWS], class_out, preferred_element_type=jnp.float32
    ).astype(jnp.bfloat16)
    combined = lax.all_to_all(
        returned.reshape(BLOCKS, PER_CLASS, width), DP, split_axis=0, concat_axis=0, tiled=True
    )
    return final_rows(summed, combined, mix)


def solution(mesh):
    fine = Mesh(mesh.devices.reshape(4, 2, 2, 4, 4, 2), (*DP, *TENSOR))
    in_specs = (
        P(DP, TENSOR),
        P(DP, TENSOR),
        P(DP, None, TENSOR),
        P(DP, None, TENSOR),
        P(DP),
        P(TENSOR),
        P(DP, None),
        P(DP, None),
        P(TENSOR, DP),
        P(DP, TENSOR),
    )
    return jax.shard_map(shards, mesh=fine, in_specs=in_specs, out_specs=P(DP, TENSOR), check_vma=False)
```

```python
import jax
import jax.numpy as jnp
from jax import lax
from jax.experimental import pallas as pl
from jax.experimental.pallas import tpu as pltpu
from jax.sharding import Mesh, PartitionSpec as P

HEADS = 48
KV = 8
HEAD = 128
D = 6144
EXPERTS = 8
TOPK = 2
CACHE = 128
SRC_CAP = 16
BLOCKS = 64
CLASSES = 4
PER_CLASS = SRC_CAP // CLASSES
CAPACITY = 384
CLASS_ROWS = CAPACITY // CLASSES + BLOCKS * 6 // (4 * CLASSES)
META = 128
ROWS = CAPACITY
SLOT_ROWS = CAPACITY // CLASSES
SQUARES = 16
UNIT = 128
LINES = ROWS // UNIT

NORM_EPSILON = 1e-05

DP = ("x", "zh", "zq", "zn")
TENSOR = ("y", "core")


TOKENS = 32
STEP = 32
GROUP = HEADS // KV


def ranks(ids):
    experts = lax.broadcasted_iota(jnp.int32, (EXPERTS, TOKENS), 0)
    names = [(ids[k : k + 1] == experts).astype(jnp.float32) for k in range(TOPK)]
    named = names[0] + names[1]
    before = lax.broadcasted_iota(jnp.int32, (TOKENS, TOKENS), 0) < lax.broadcasted_iota(
        jnp.int32, (TOKENS, TOKENS), 1
    )
    earlier = jnp.dot(named, before.astype(jnp.float32), preferred_element_type=jnp.float32)
    rank = [jnp.sum(earlier * name, axis=0, keepdims=True).astype(jnp.int32) for name in names]
    return names, rank, named


def slot_iota():
    return lax.broadcasted_iota(jnp.int32, (EXPERTS * SRC_CAP, TOKENS), 0)


def packet_place(ids, rank, turn):
    return ids * SRC_CAP + (rank + turn) % CLASSES * PER_CLASS + rank // CLASSES


def tokens_kernel(
    block_ref, lengths_ref, ids_ref, residual_ref, queries_ref, keys_ref, values_ref,
    summed_ref, out_ref, query_ref, attended_ref, all_ref,
):
    step = pl.program_id(0)

    @pl.when(step == 0)
    def _():
        query_ref[...] = jnp.zeros_like(query_ref)

    for h in range(GROUP):
        query_ref[:, h, :] = queries_ref[:, h * HEAD : (h + 1) * HEAD].astype(jnp.float32)
    position = lax.broadcasted_iota(jnp.int32, (8, CACHE), 1)
    scores = []
    for t in range(STEP):
        products = lax.dot_general(
            query_ref[t].astype(jnp.bfloat16),
            keys_ref[t],
            (((1,), (1,)), ((), ())),
            preferred_element_type=jnp.float32,
        ) * HEAD ** (-0.5)
        scores.append(jnp.where(position < lengths_ref[step * STEP + t], products, -1e30))
    scores = jnp.concatenate(scores, axis=0)
    powered = jnp.exp(scores - jnp.max(scores, axis=1, keepdims=True))
    probs = powered / jnp.sum(powered, axis=1, keepdims=True)
    for t in range(STEP):
        attended_ref[t] = jnp.dot(
            probs[t * 8 : (t + 1) * 8].astype(jnp.bfloat16), values_ref[t], preferred_element_type=jnp.float32
        )
    for h in range(GROUP):
        lanes = slice(h * HEAD, (h + 1) * HEAD)
        total = residual_ref[:, lanes].astype(jnp.float32) + attended_ref[:, h, :]
        summed_ref[:, lanes] = total
        all_ref[pl.ds(pl.multiple_of(step * STEP, STEP), STEP), lanes] = total

    @pl.when(step == TOKENS // STEP - 1)
    def _():
        ids = ids_ref[...]
        _, rank, named = ranks(ids)
        pick = jnp.zeros((EXPERTS * SRC_CAP, TOKENS), jnp.float32)
        for k in range(TOPK):
            pick = jnp.where(slot_iota() == packet_place(ids[k : k + 1], rank[k], block_ref[0]), 1.0, pick)
        packed = jnp.dot(
            pick.astype(jnp.bfloat16), all_ref[...].astype(jnp.bfloat16), preferred_element_type=jnp.float32
        )
        width = packed.shape[1]
        own_lane = lax.broadcasted_iota(jnp.int32, (EXPERTS, META), 0) == lax.broadcasted_iota(
            jnp.int32, (EXPERTS, META), 1
        )
        counts = jnp.sum(named, axis=1, keepdims=True)
        counts = jnp.sum(jnp.where(own_lane, counts, 0.0), axis=0, keepdims=True)
        meta = jnp.broadcast_to(counts, (PER_CLASS, META)).astype(jnp.bfloat16)
        for e in range(EXPERTS):
            for c in range(CLASSES):
                first = e * SRC_CAP + c * PER_CLASS
                rows = packed[first : first + PER_CLASS].astype(jnp.bfloat16)
                for group in range(2):
                    peer = (e * 2 + group) * CLASSES + c
                    out_ref[peer, :, :width] = rows
                    out_ref[peer, :, width:] = meta


def tokens_packed(block, lengths, expert_ids, residual, queries, keys, values):
    tokens, width = residual.shape
    whole = lambda *shape: pl.BlockSpec(shape, lambda i: (0,) * len(shape))
    return pl.pallas_call(
        tokens_kernel,
        grid=(TOKENS // STEP,),
        in_specs=[
            pl.BlockSpec(memory_space=pltpu.SMEM),
            pl.BlockSpec(memory_space=pltpu.SMEM),
            whole(TOPK, TOKENS),
            pl.BlockSpec((STEP, width), lambda i: (i, 0)),
            pl.BlockSpec((STEP, width), lambda i: (i, 0)),
            pl.BlockSpec((STEP, CACHE, HEAD), lambda i: (i, 0, 0)),
            pl.BlockSpec((STEP, CACHE, HEAD), lambda i: (i, 0, 0)),
        ],
        out_specs=[
            pl.BlockSpec((STEP, width), lambda i: (i, 0)),
            whole(BLOCKS, PER_CLASS, width + META),
        ],
        out_shape=[
            jax.ShapeDtypeStruct((tokens, width), jnp.float32),
            jax.ShapeDtypeStruct((BLOCKS, PER_CLASS, width + META), jnp.bfloat16),
        ],
        scratch_shapes=[
            pltpu.VMEM((STEP, 8, HEAD), jnp.float32),
            pltpu.VMEM((STEP, 8, HEAD), jnp.float32),
            pltpu.VMEM((TOKENS, width), jnp.float32),
        ],
        compiler_params=pltpu.CompilerParams(vmem_limit_bytes=10 << 20),
        name="tokens_packed",
    )(
        block.reshape(1),
        *(
            pltpu.with_memory_space_constraint(operand, pltpu.HBM)
            for operand in (lengths, expert_ids.T, residual, queries, keys, values)
        ),
    )


def summed_at_owner(pieces, axis):
    return jnp.sum(
        lax.all_to_all(pieces, axis, split_axis=0, concat_axis=0, tiled=True).astype(jnp.float32), axis=0
    )


def diagonal():
    row = lax.broadcasted_iota(jnp.int32, (UNIT, UNIT), 0)
    return row == lax.broadcasted_iota(jnp.int32, (UNIT, UNIT), 1)


def leading_and_rest(sums):
    leading = sums.astype(jnp.bfloat16)
    return jnp.concatenate([leading, (sums - leading.astype(jnp.float32)).astype(jnp.bfloat16)], axis=0)


def write_pieces(rows, squares, w_ref, half, out_ref):
    columns = 2 * UNIT
    for k in range(2):
        source = (half * 2 + k) * columns
        parts = jnp.dot(
            rows,
            w_ref[:, pl.ds(pl.multiple_of(source, columns), columns)],
            preferred_element_type=jnp.float32,
        )
        for side in range(2):
            piece = k * 2 + side
            out_ref[piece, :ROWS] = parts[:, side * UNIT : (side + 1) * UNIT].astype(jnp.bfloat16)
            out_ref[piece, ROWS:] = squares


def sent_kernel(core_ref, place_ref, gathered_ref, w_ref, send_ref, rows_ref, squares_ref):
    wide = lax.dot_general(
        place_ref[...], gathered_ref[...], (((0,), (0,)), ((), ())), preferred_element_type=jnp.float32
    )
    rows = wide.astype(jnp.bfloat16)
    rows_ref[...] = rows
    sums = jnp.sum(wide * wide, axis=1, keepdims=True)
    lines = [
        jnp.sum(jnp.where(diagonal(), sums[g * UNIT : (g + 1) * UNIT], 0.0), axis=0, keepdims=True)
        for g in range(LINES)
    ]
    lines.append(jnp.zeros((SQUARES // 2 - LINES, UNIT), jnp.float32))
    squares = leading_and_rest(jnp.concatenate(lines, axis=0))
    squares_ref[...] = squares
    write_pieces(rows, squares, w_ref, 1 - core_ref[0], send_ref)


def kept_kernel(core_ref, rows_ref, squares_ref, w_ref, keep_ref):
    write_pieces(rows_ref[...], squares_ref[...], w_ref, core_ref[0], keep_ref)


def first_product(kernel, name, out_shape, core, *operands):
    return pl.pallas_call(
        kernel,
        in_specs=[
            pl.BlockSpec(memory_space=pltpu.SMEM),
            *[pl.BlockSpec(memory_space=pltpu.VMEM)] * len(operands),
        ],
        out_shape=out_shape,
        compiler_params=pltpu.CompilerParams(vmem_limit_bytes=10 << 20),
        name=name,
    )(core.reshape(1), *operands)


def half_of_units(w_in):
    return jax.ShapeDtypeStruct((w_in.shape[1] // (2 * UNIT), ROWS + SQUARES, UNIT), jnp.bfloat16)


def sent_pieces(place, gathered, w_in, core):
    out_shape = [
        half_of_units(w_in),
        jax.ShapeDtypeStruct((ROWS, gathered.shape[1]), jnp.bfloat16),
        jax.ShapeDtypeStruct((SQUARES, UNIT), jnp.bfloat16),
    ]
    return first_product(sent_kernel, "sent_pieces", out_shape, core, place, gathered, w_in)


def kept_pieces(rows, squares, w_in, core):
    return first_product(kept_kernel, "kept_pieces", half_of_units(w_in), core, rows, squares, w_in)


def core_kernel(own_ref, other_ref, out_ref):
    out_ref[:, :ROWS] = (
        own_ref[:, :ROWS].astype(jnp.float32) + other_ref[:, :ROWS].astype(jnp.float32)
    ).astype(jnp.bfloat16)
    both = own_ref[0, ROWS:].astype(jnp.float32) + other_ref[0, ROWS:].astype(jnp.float32)
    split = leading_and_rest(both[: SQUARES // 2] + both[SQUARES // 2 :])
    for piece in range(out_ref.shape[0]):
        out_ref[piece, ROWS:] = split


def core_summed(own, other):
    return pl.pallas_call(
        core_kernel,
        out_shape=jax.ShapeDtypeStruct(own.shape, jnp.bfloat16),
        compiler_params=pltpu.CompilerParams(vmem_limit_bytes=10 << 20),
        name="core_summed",
    )(own, other)


def silu_kernel(in_ref, out_ref):
    total = in_ref[0].astype(jnp.float32)
    for piece in range(1, in_ref.shape[0]):
        total = total + in_ref[piece].astype(jnp.float32)
    squares = total[ROWS : ROWS + SQUARES // 2] + total[ROWS + SQUARES // 2 :]
    for g in range(LINES):
        own = jnp.sum(jnp.where(diagonal(), squares[g : g + 1], 0.0), axis=1, keepdims=True)
        scaled = total[g * UNIT : (g + 1) * UNIT] * lax.rsqrt(own / D + NORM_EPSILON)
        hidden = (scaled / (1.0 + jnp.exp(-scaled))).astype(jnp.bfloat16)
        for piece in range(out_ref.shape[0]):
            out_ref[piece, g * UNIT : (g + 1) * UNIT] = hidden


def silu_copies(pieces):
    return pl.pallas_call(
        silu_kernel,
        out_shape=jax.ShapeDtypeStruct((pieces.shape[0], ROWS, UNIT), jnp.bfloat16),
        compiler_params=pltpu.CompilerParams(vmem_limit_bytes=10 << 20),
        name="silu_copies",
    )(pieces)


def output_kernel(hidden_ref, w_ref, out_ref):
    hidden = jnp.concatenate([hidden_ref[piece] for piece in range(hidden_ref.shape[0])], axis=1)
    out_ref[...] = jnp.dot(hidden, w_ref[...], preferred_element_type=jnp.float32).astype(jnp.bfloat16)


def output_parts(hidden, w_out):
    return pl.pallas_call(
        output_kernel,
        in_specs=[pl.BlockSpec(memory_space=pltpu.VMEM)] * 2,
        out_shape=jax.ShapeDtypeStruct((ROWS, w_out.shape[1]), jnp.bfloat16),
        compiler_params=pltpu.CompilerParams(vmem_limit_bytes=10 << 20),
        name="output_parts",
    )(hidden, w_out)


def flags(condition):
    return condition.astype(jnp.float32).astype(jnp.bfloat16)


def kept_of_blocks(all_counts, own_block):
    slots = all_counts.shape[0]
    row = lax.broadcasted_iota(jnp.int32, (slots, slots), 0)
    column = lax.broadcasted_iota(jnp.int32, (slots, slots), 1)
    earlier = flags(((column & 3) == 0) & (column < (row & -4)))

    def earlier_sum(counts):
        return jnp.dot(earlier, counts, preferred_element_type=jnp.float32).astype(jnp.int32)

    own_expert = own_block >> 3
    counts = jnp.dot(
        all_counts,
        flags(lax.broadcasted_iota(jnp.int32, (META, META), 0) == own_expert),
        preferred_element_type=jnp.float32,
    )
    offset = earlier_sum(counts.astype(jnp.bfloat16))
    return offset, jnp.clip(CAPACITY - offset, 0, counts.astype(jnp.int32)), earlier_sum


def compact_kernel(here_ref, received_ref, rows_ref, place_ref, counts_ref):
    width = rows_ref.shape[1]
    own_class = here_ref[1]
    received = received_ref[...].reshape(BLOCKS * PER_CLASS, width + META)
    all_counts = received[:, width:]
    counts_ref[...] = all_counts
    offset, kept, earlier_sum = kept_of_blocks(all_counts, here_ref[0])
    line = lax.broadcasted_iota(jnp.int32, kept.shape, 0)
    lane = lax.broadcasted_iota(jnp.int32, kept.shape, 1)
    block, place = line >> 2, line & 3

    shift = (own_class + (lane >> 5) + BLOCKS - block) & 3
    in_class = (kept - shift + 3) >> 2
    first = earlier_sum(in_class.astype(jnp.float32).astype(jnp.bfloat16))
    live = place < in_class
    spot = jnp.where(live, first + place, -1)
    slot = jnp.where(live, offset + place * 4 + shift + 1, 0)
    digits = jnp.where((lane & 16) == 0, slot >> 4, slot & 15).astype(jnp.float32).astype(jnp.bfloat16)

    for turn in range(CLASSES):
        start = turn * 32
        chosen = flags(spot[:, start : start + 1] == lane)
        if turn == 0:
            rows = lax.dot_general(
                chosen, received[:, :width], (((0,), (0,)), ((), ())), preferred_element_type=jnp.float32
            )
            rows_ref[...] = rows[:CLASS_ROWS].astype(jnp.bfloat16)
        found = lax.dot_general(chosen, digits, (((0,), (0,)), ((), ())), preferred_element_type=jnp.float32)
        found = found[:CLASS_ROWS, start : start + 1] * 16.0 + found[:CLASS_ROWS, start + 16 : start + 17]
        found = found.astype(jnp.int32) - 1
        target = jnp.where(found < 0, -1, (found & 3) * SLOT_ROWS + (found >> 2))
        of_class = (own_class + turn) & 3
        place_ref[pl.ds(pl.multiple_of(of_class * CLASS_ROWS, 8), CLASS_ROWS)] = flags(
            target == lax.broadcasted_iota(jnp.int32, (CLASS_ROWS, ROWS), 1)
        )


def compacted(received, own_block, own_class):
    blocks, places, wide = received.shape
    return pl.pallas_call(
        compact_kernel,
        in_specs=[
            pl.BlockSpec(memory_space=pltpu.SMEM),
            pl.BlockSpec(memory_space=pltpu.VMEM),
        ],
        out_shape=[
            jax.ShapeDtypeStruct((CLASS_ROWS, wide - META), jnp.bfloat16),
            jax.ShapeDtypeStruct((CLASSES * CLASS_ROWS, ROWS), jnp.bfloat16),
            jax.ShapeDtypeStruct((blocks * places, META), jnp.bfloat16),
        ],
        compiler_params=pltpu.CompilerParams(vmem_limit_bytes=10 << 20),
        name="compacted",
    )(jnp.stack([own_block, own_class]), received)


def back_kernel(here_ref, ids_ref, weights_ref, counts_ref, back_ref, mix_ref):
    own_block, own_class = here_ref[0], here_ref[1]
    all_counts = counts_ref[...]
    offset, kept, _ = kept_of_blocks(all_counts, own_block)
    line = lax.broadcasted_iota(jnp.int32, kept.shape, 0)
    lane = lax.broadcasted_iota(jnp.int32, kept.shape, 1)
    block, place = line >> 2, line & 3
    rank = place * 4 + ((own_class - offset) & 3)
    back_ref[...] = flags(((offset + rank - own_class) >> 2 == lane) & (rank < kept))

    ids = ids_ref[...]
    names, rank, _ = ranks(ids)
    offsets = lax.dot_general(
        all_counts,
        flags((block < own_block) & (place == 0)),
        (((0,), (0,)), ((), ())),
        preferred_element_type=jnp.float32,
    )[:EXPERTS, :TOKENS]
    mix = jnp.zeros((EXPERTS * SRC_CAP, TOKENS), jnp.float32)
    for k in range(TOPK):
        turn = jnp.sum(offsets * names[k], axis=0, keepdims=True).astype(jnp.int32)
        mix = jnp.where(
            slot_iota() == packet_place(ids[k : k + 1], rank[k], turn), weights_ref[k : k + 1], mix
        )
    for part in range(3):
        rounded = mix.astype(jnp.bfloat16)
        for e in range(EXPERTS):
            for group in range(2):
                first = (e * 2 + group) * SRC_CAP
                mix_ref[part, first : first + SRC_CAP] = rounded[e * SRC_CAP : (e + 1) * SRC_CAP]
        mix = mix - rounded.astype(jnp.float32)


def way_back(counts, own_block, own_class, expert_ids, expert_weights):
    return pl.pallas_call(
        back_kernel,
        in_specs=[
            pl.BlockSpec(memory_space=pltpu.SMEM),
            pl.BlockSpec(memory_space=pltpu.VMEM),
            pl.BlockSpec(memory_space=pltpu.VMEM),
            pl.BlockSpec(memory_space=pltpu.VMEM),
        ],
        out_shape=[
            jax.ShapeDtypeStruct(counts.shape, jnp.bfloat16),
            jax.ShapeDtypeStruct((3, 2 * EXPERTS * SRC_CAP, TOKENS), jnp.bfloat16),
        ],
        compiler_params=pltpu.CompilerParams(vmem_limit_bytes=10 << 20),
        name="way_back",
    )(jnp.stack([own_block, own_class]), expert_ids.T, expert_weights.T, counts)


def final_kernel(summed_ref, combined_ref, mix_ref, out_ref):
    total = summed_ref[...]
    rows = combined_ref[...].reshape(BLOCKS * PER_CLASS, total.shape[1])
    for part in (2, 1, 0):
        total = total + lax.dot_general(
            mix_ref[part], rows, (((0,), (0,)), ((), ())), preferred_element_type=jnp.float32
        )
    out_ref[...] = total.astype(jnp.bfloat16)


def final_rows(summed, combined, mix):
    return pl.pallas_call(
        final_kernel,
        in_specs=[pl.BlockSpec(memory_space=pltpu.VMEM)] * 3,
        out_shape=jax.ShapeDtypeStruct(summed.shape, jnp.bfloat16),
        compiler_params=pltpu.CompilerParams(vmem_limit_bytes=10 << 20),
        name="final_rows",
    )(summed, combined, mix)


def shards(
    residual, queries, keys, values, lengths, norm_gain, expert_ids, expert_weights, w_in, w_out
):
    tokens, width = residual.shape
    block = ((lax.axis_index("x") * 2 + lax.axis_index("zh")) * 2 + lax.axis_index("zq")) * 4 + lax.axis_index("zn")
    own_class = lax.axis_index("zn")

    summed, outgoing = tokens_packed(block, lengths, expert_ids, residual, queries, keys, values)
    gained = (w_in.astype(jnp.float32) * norm_gain.astype(jnp.float32)[:, None]).astype(jnp.bfloat16)
    received = lax.all_to_all(outgoing, DP, split_axis=0, concat_axis=0, tiled=True)
    class_rows, place, counts = compacted(received, block, own_class)
    rows = lax.all_gather(class_rows, "zn", axis=0, tiled=True)
    core = lax.axis_index("core")
    send, rows, squares = sent_pieces(place, rows, gained, core)
    other = lax.ppermute(send, "core", ((0, 1), (1, 0)))
    own = kept_pieces(rows, squares, gained, core)
    counts, squares = lax.optimization_barrier((counts, squares))
    back, mix = way_back(counts, block, own_class, expert_ids, expert_weights)
    own, back, mix = lax.optimization_barrier((own, back, mix))
    pieces = lax.all_to_all(core_summed(own, other), "y", split_axis=0, concat_axis=0, tiled=True)
    gathered = lax.all_to_all(silu_copies(pieces), "y", split_axis=0, concat_axis=0, tiled=True)
    gathered = lax.all_gather(gathered, "core", axis=0, tiled=True)
    results = output_parts(gathered, w_out)

    class_out = summed_at_owner(results.reshape(CLASSES, SLOT_ROWS, width), "zn").astype(jnp.bfloat16)
    returned = jnp.dot(
        back[:, :SLOT_ROWS], class_out, preferred_element_type=jnp.float32
    ).astype(jnp.bfloat16)
    combined = lax.all_to_all(
        returned.reshape(BLOCKS, PER_CLASS, width), DP, split_axis=0, concat_axis=0, tiled=True
    )
    return final_rows(summed, combined, mix)


def solution(mesh):
    fine = Mesh(mesh.devices.reshape(4, 2, 2, 4, 4, 2), (*DP, *TENSOR))
    in_specs = (
        P(DP, TENSOR),
        P(DP, TENSOR),
        P(DP, None, TENSOR),
        P(DP, None, TENSOR),
        P(DP),
        P(TENSOR),
        P(DP, None),
        P(DP, None),
        P(TENSOR, DP),
        P(DP, TENSOR),
    )
    return jax.shard_map(shards, mesh=fine, in_specs=in_specs, out_specs=P(DP, TENSOR), check_vma=False)
```

```python
import jax
import jax.numpy as jnp
from jax import lax
from jax.experimental import pallas as pl
from jax.experimental.pallas import tpu as pltpu
from jax.sharding import Mesh, PartitionSpec as P

HEADS = 48
KV = 8
HEAD = 128
D = 6144
EXPERTS = 8
TOPK = 2
CACHE = 128
SRC_CAP = 16
BLOCKS = 64
CLASSES = 4
PER_CLASS = SRC_CAP // CLASSES
CAPACITY = 384
CLASS_ROWS = CAPACITY // CLASSES + BLOCKS * 6 // (4 * CLASSES)
META = 128
ROWS = CAPACITY
SLOT_ROWS = CAPACITY // CLASSES
SQUARES = 16
UNIT = 128
LINES = ROWS // UNIT

NORM_EPSILON = 1e-05

DP = ("x", "zh", "zq", "zn")
TENSOR = ("y", "core")


TOKENS = 32
STEP = 32
GROUP = HEADS // KV


def ranks(ids):
    experts = lax.broadcasted_iota(jnp.int32, (EXPERTS, TOKENS), 0)
    names = [(ids[k : k + 1] == experts).astype(jnp.float32) for k in range(TOPK)]
    named = names[0] + names[1]
    before = lax.broadcasted_iota(jnp.int32, (TOKENS, TOKENS), 0) < lax.broadcasted_iota(
        jnp.int32, (TOKENS, TOKENS), 1
    )
    earlier = jnp.dot(named, before.astype(jnp.float32), preferred_element_type=jnp.float32)
    rank = [jnp.sum(earlier * name, axis=0, keepdims=True).astype(jnp.int32) for name in names]
    return names, rank, named


def slot_iota():
    return lax.broadcasted_iota(jnp.int32, (EXPERTS * SRC_CAP, TOKENS), 0)


def packet_place(ids, rank, turn):
    return ids * SRC_CAP + (rank + turn) % CLASSES * PER_CLASS + rank // CLASSES


def tokens_kernel(
    block_ref, lengths_ref, ids_ref, residual_ref, queries_ref, keys_ref, values_ref,
    summed_ref, out_ref, query_ref, attended_ref, all_ref,
):
    step = pl.program_id(0)

    @pl.when(step == 0)
    def _():
        query_ref[...] = jnp.zeros_like(query_ref)

    for h in range(GROUP):
        query_ref[:, h, :] = queries_ref[:, h * HEAD : (h + 1) * HEAD].astype(jnp.float32)
    position = lax.broadcasted_iota(jnp.int32, (8, CACHE), 1)
    scores = []
    for t in range(STEP):
        products = lax.dot_general(
            query_ref[t].astype(jnp.bfloat16),
            keys_ref[t],
            (((1,), (1,)), ((), ())),
            preferred_element_type=jnp.float32,
        ) * HEAD ** (-0.5)
        scores.append(jnp.where(position < lengths_ref[step * STEP + t], products, -1e30))
    scores = jnp.concatenate(scores, axis=0)
    powered = jnp.exp(scores - jnp.max(scores, axis=1, keepdims=True))
    probs = powered / jnp.sum(powered, axis=1, keepdims=True)
    for t in range(STEP):
        attended_ref[t] = jnp.dot(
            probs[t * 8 : (t + 1) * 8].astype(jnp.bfloat16), values_ref[t], preferred_element_type=jnp.float32
        )
    for h in range(GROUP):
        lanes = slice(h * HEAD, (h + 1) * HEAD)
        total = residual_ref[:, lanes].astype(jnp.float32) + attended_ref[:, h, :]
        summed_ref[:, lanes] = total
        all_ref[pl.ds(pl.multiple_of(step * STEP, STEP), STEP), lanes] = total

    @pl.when(step == TOKENS // STEP - 1)
    def _():
        ids = ids_ref[...]
        _, rank, named = ranks(ids)
        pick = jnp.zeros((EXPERTS * SRC_CAP, TOKENS), jnp.float32)
        for k in range(TOPK):
            pick = jnp.where(slot_iota() == packet_place(ids[k : k + 1], rank[k], block_ref[0]), 1.0, pick)
        packed = jnp.dot(
            pick.astype(jnp.bfloat16), all_ref[...].astype(jnp.bfloat16), preferred_element_type=jnp.float32
        )
        width = packed.shape[1]
        own_lane = lax.broadcasted_iota(jnp.int32, (EXPERTS, META), 0) == lax.broadcasted_iota(
            jnp.int32, (EXPERTS, META), 1
        )
        counts = jnp.sum(named, axis=1, keepdims=True)
        counts = jnp.sum(jnp.where(own_lane, counts, 0.0), axis=0, keepdims=True)
        meta = jnp.broadcast_to(counts, (PER_CLASS, META)).astype(jnp.bfloat16)
        for e in range(EXPERTS):
            for c in range(CLASSES):
                first = e * SRC_CAP + c * PER_CLASS
                rows = packed[first : first + PER_CLASS].astype(jnp.bfloat16)
                for group in range(2):
                    peer = (e * 2 + group) * CLASSES + c
                    out_ref[peer, :, :width] = rows
                    out_ref[peer, :, width:] = meta


def tokens_packed(block, lengths, expert_ids, residual, queries, keys, values):
    tokens, width = residual.shape
    whole = lambda *shape: pl.BlockSpec(shape, lambda i: (0,) * len(shape))
    return pl.pallas_call(
        tokens_kernel,
        grid=(TOKENS // STEP,),
        in_specs=[
            pl.BlockSpec(memory_space=pltpu.SMEM),
            pl.BlockSpec(memory_space=pltpu.SMEM),
            whole(TOPK, TOKENS),
            pl.BlockSpec((STEP, width), lambda i: (i, 0)),
            pl.BlockSpec((STEP, width), lambda i: (i, 0)),
            pl.BlockSpec((STEP, CACHE, HEAD), lambda i: (i, 0, 0)),
            pl.BlockSpec((STEP, CACHE, HEAD), lambda i: (i, 0, 0)),
        ],
        out_specs=[
            pl.BlockSpec((STEP, width), lambda i: (i, 0)),
            whole(BLOCKS, PER_CLASS, width + META),
        ],
        out_shape=[
            jax.ShapeDtypeStruct((tokens, width), jnp.float32),
            jax.ShapeDtypeStruct((BLOCKS, PER_CLASS, width + META), jnp.bfloat16),
        ],
        scratch_shapes=[
            pltpu.VMEM((STEP, 8, HEAD), jnp.float32),
            pltpu.VMEM((STEP, 8, HEAD), jnp.float32),
            pltpu.VMEM((TOKENS, width), jnp.float32),
        ],
        compiler_params=pltpu.CompilerParams(vmem_limit_bytes=10 << 20),
        name="tokens_packed",
    )(
        block.reshape(1),
        *(
            pltpu.with_memory_space_constraint(operand, pltpu.HBM)
            for operand in (lengths, expert_ids.T, residual, queries, keys, values)
        ),
    )


def diagonal():
    row = lax.broadcasted_iota(jnp.int32, (UNIT, UNIT), 0)
    return row == lax.broadcasted_iota(jnp.int32, (UNIT, UNIT), 1)


def leading_and_rest(sums):
    leading = sums.astype(jnp.bfloat16)
    return jnp.concatenate([leading, (sums - leading.astype(jnp.float32)).astype(jnp.bfloat16)], axis=0)


def write_pieces(rows, squares, w_ref, half, out_ref):
    columns = 2 * UNIT
    for k in range(2):
        source = (half * 2 + k) * columns
        parts = jnp.dot(
            rows,
            w_ref[:, pl.ds(pl.multiple_of(source, columns), columns)],
            preferred_element_type=jnp.float32,
        )
        for side in range(2):
            piece = k * 2 + side
            out_ref[piece, :ROWS] = parts[:, side * UNIT : (side + 1) * UNIT].astype(jnp.bfloat16)
            out_ref[piece, ROWS:] = squares


def sent_kernel(core_ref, place_ref, gathered_ref, w_ref, send_ref, rows_ref, squares_ref):
    wide = lax.dot_general(
        place_ref[...], gathered_ref[...], (((0,), (0,)), ((), ())), preferred_element_type=jnp.float32
    )
    rows = wide.astype(jnp.bfloat16)
    rows_ref[...] = rows
    sums = jnp.sum(wide * wide, axis=1, keepdims=True)
    lines = [
        jnp.sum(jnp.where(diagonal(), sums[g * UNIT : (g + 1) * UNIT], 0.0), axis=0, keepdims=True)
        for g in range(LINES)
    ]
    lines.append(jnp.zeros((SQUARES // 2 - LINES, UNIT), jnp.float32))
    squares = leading_and_rest(jnp.concatenate(lines, axis=0))
    squares_ref[...] = squares
    write_pieces(rows, squares, w_ref, 1 - core_ref[0], send_ref)


def kept_kernel(core_ref, rows_ref, squares_ref, w_ref, keep_ref):
    write_pieces(rows_ref[...], squares_ref[...], w_ref, core_ref[0], keep_ref)


def first_product(kernel, name, out_shape, core, *operands):
    return pl.pallas_call(
        kernel,
        in_specs=[
            pl.BlockSpec(memory_space=pltpu.SMEM),
            *[pl.BlockSpec(memory_space=pltpu.VMEM)] * len(operands),
        ],
        out_shape=out_shape,
        compiler_params=pltpu.CompilerParams(vmem_limit_bytes=10 << 20),
        name=name,
    )(core.reshape(1), *operands)


def half_of_units(w_in):
    return jax.ShapeDtypeStruct((w_in.shape[1] // (2 * UNIT), ROWS + SQUARES, UNIT), jnp.bfloat16)


def sent_pieces(place, gathered, w_in, core):
    out_shape = [
        half_of_units(w_in),
        jax.ShapeDtypeStruct((ROWS, gathered.shape[1]), jnp.bfloat16),
        jax.ShapeDtypeStruct((SQUARES, UNIT), jnp.bfloat16),
    ]
    return first_product(sent_kernel, "sent_pieces", out_shape, core, place, gathered, w_in)


def kept_pieces(rows, squares, w_in, core):
    return first_product(kept_kernel, "kept_pieces", half_of_units(w_in), core, rows, squares, w_in)


def core_kernel(own_ref, other_ref, out_ref):
    out_ref[:, :ROWS] = (
        own_ref[:, :ROWS].astype(jnp.float32) + other_ref[:, :ROWS].astype(jnp.float32)
    ).astype(jnp.bfloat16)
    both = own_ref[0, ROWS:].astype(jnp.float32) + other_ref[0, ROWS:].astype(jnp.float32)
    split = leading_and_rest(both[: SQUARES // 2] + both[SQUARES // 2 :])
    for piece in range(out_ref.shape[0]):
        out_ref[piece, ROWS:] = split


def core_summed(own, other):
    return pl.pallas_call(
        core_kernel,
        out_shape=jax.ShapeDtypeStruct(own.shape, jnp.bfloat16),
        compiler_params=pltpu.CompilerParams(vmem_limit_bytes=10 << 20),
        name="core_summed",
    )(own, other)


def silu_kernel(in_ref, out_ref):
    total = in_ref[0].astype(jnp.float32)
    for piece in range(1, in_ref.shape[0]):
        total = total + in_ref[piece].astype(jnp.float32)
    squares = total[ROWS : ROWS + SQUARES // 2] + total[ROWS + SQUARES // 2 :]
    for g in range(LINES):
        own = jnp.sum(jnp.where(diagonal(), squares[g : g + 1], 0.0), axis=1, keepdims=True)
        scaled = total[g * UNIT : (g + 1) * UNIT] * lax.rsqrt(own / D + NORM_EPSILON)
        hidden = (scaled / (1.0 + jnp.exp(-scaled))).astype(jnp.bfloat16)
        for piece in range(out_ref.shape[0]):
            out_ref[piece, g * UNIT : (g + 1) * UNIT] = hidden


def silu_copies(pieces):
    return pl.pallas_call(
        silu_kernel,
        out_shape=jax.ShapeDtypeStruct((pieces.shape[0], ROWS, UNIT), jnp.bfloat16),
        compiler_params=pltpu.CompilerParams(vmem_limit_bytes=10 << 20),
        name="silu_copies",
    )(pieces)


def output_kernel(class_ref, hidden_ref, w_ref, *out_refs):
    for k, out_ref in enumerate(out_refs):
        rows = pl.ds(pl.multiple_of((class_ref[0] ^ k) * SLOT_ROWS, SLOT_ROWS), SLOT_ROWS)
        hidden = jnp.concatenate([hidden_ref[piece, rows] for piece in range(hidden_ref.shape[0])], axis=1)
        out_ref[...] = jnp.dot(hidden, w_ref[...], preferred_element_type=jnp.float32).astype(jnp.bfloat16)


def output_parts(hidden, w_out, own_class):
    part = jax.ShapeDtypeStruct((SLOT_ROWS, w_out.shape[1]), jnp.bfloat16)
    return pl.pallas_call(
        output_kernel,
        in_specs=[
            pl.BlockSpec(memory_space=pltpu.SMEM),
            pl.BlockSpec(memory_space=pltpu.VMEM),
            pl.BlockSpec(memory_space=pltpu.VMEM),
        ],
        out_shape=[part] * CLASSES,
        compiler_params=pltpu.CompilerParams(vmem_limit_bytes=10 << 20),
        name="output_parts",
    )(own_class.reshape(1), hidden, w_out)


def flags(condition):
    return condition.astype(jnp.float32).astype(jnp.bfloat16)


def kept_of_blocks(all_counts, own_block):
    slots = all_counts.shape[0]
    row = lax.broadcasted_iota(jnp.int32, (slots, slots), 0)
    column = lax.broadcasted_iota(jnp.int32, (slots, slots), 1)
    earlier = flags(((column & 3) == 0) & (column < (row & -4)))

    def earlier_sum(counts):
        return jnp.dot(earlier, counts, preferred_element_type=jnp.float32).astype(jnp.int32)

    own_expert = own_block >> 3
    counts = jnp.dot(
        all_counts,
        flags(lax.broadcasted_iota(jnp.int32, (META, META), 0) == own_expert),
        preferred_element_type=jnp.float32,
    )
    offset = earlier_sum(counts.astype(jnp.bfloat16))
    return offset, jnp.clip(CAPACITY - offset, 0, counts.astype(jnp.int32)), earlier_sum


def compact_kernel(here_ref, received_ref, rows_ref, place_ref, counts_ref):
    width = rows_ref.shape[1]
    own_class = here_ref[1]
    received = received_ref[...].reshape(BLOCKS * PER_CLASS, width + META)
    all_counts = received[:, width:]
    counts_ref[...] = all_counts
    offset, kept, earlier_sum = kept_of_blocks(all_counts, here_ref[0])
    line = lax.broadcasted_iota(jnp.int32, kept.shape, 0)
    lane = lax.broadcasted_iota(jnp.int32, kept.shape, 1)
    block, place = line >> 2, line & 3

    shift = (own_class + (lane >> 5) + BLOCKS - block) & 3
    in_class = (kept - shift + 3) >> 2
    first = earlier_sum(in_class.astype(jnp.float32).astype(jnp.bfloat16))
    live = place < in_class
    spot = jnp.where(live, first + place, -1)
    slot = jnp.where(live, offset + place * 4 + shift + 1, 0)
    digits = jnp.where((lane & 16) == 0, slot >> 4, slot & 15).astype(jnp.float32).astype(jnp.bfloat16)

    for turn in range(CLASSES):
        start = turn * 32
        chosen = flags(spot[:, start : start + 1] == lane)
        if turn == 0:
            rows = lax.dot_general(
                chosen, received[:, :width], (((0,), (0,)), ((), ())), preferred_element_type=jnp.float32
            )
            rows_ref[...] = rows[:CLASS_ROWS].astype(jnp.bfloat16)
        found = lax.dot_general(chosen, digits, (((0,), (0,)), ((), ())), preferred_element_type=jnp.float32)
        found = found[:CLASS_ROWS, start : start + 1] * 16.0 + found[:CLASS_ROWS, start + 16 : start + 17]
        found = found.astype(jnp.int32) - 1
        target = jnp.where(found < 0, -1, (found & 3) * SLOT_ROWS + (found >> 2))
        of_class = (own_class + turn) & 3
        place_ref[pl.ds(pl.multiple_of(of_class * CLASS_ROWS, 8), CLASS_ROWS)] = flags(
            target == lax.broadcasted_iota(jnp.int32, (CLASS_ROWS, ROWS), 1)
        )


def compacted(received, own_block, own_class):
    blocks, places, wide = received.shape
    return pl.pallas_call(
        compact_kernel,
        in_specs=[
            pl.BlockSpec(memory_space=pltpu.SMEM),
            pl.BlockSpec(memory_space=pltpu.VMEM),
        ],
        out_shape=[
            jax.ShapeDtypeStruct((CLASS_ROWS, wide - META), jnp.bfloat16),
            jax.ShapeDtypeStruct((CLASSES * CLASS_ROWS, ROWS), jnp.bfloat16),
            jax.ShapeDtypeStruct((blocks * places, META), jnp.bfloat16),
        ],
        compiler_params=pltpu.CompilerParams(vmem_limit_bytes=10 << 20),
        name="compacted",
    )(jnp.stack([own_block, own_class]), received)


def back_kernel(here_ref, ids_ref, weights_ref, counts_ref, back_ref, mix_ref):
    own_block, own_class = here_ref[0], here_ref[1]
    all_counts = counts_ref[...]
    offset, kept, _ = kept_of_blocks(all_counts, own_block)
    line = lax.broadcasted_iota(jnp.int32, kept.shape, 0)
    lane = lax.broadcasted_iota(jnp.int32, kept.shape, 1)
    block, place = line >> 2, line & 3
    rank = place * 4 + ((own_class - offset) & 3)
    back_ref[...] = flags(((offset + rank - own_class) >> 2 == lane) & (rank < kept))

    ids = ids_ref[...]
    names, rank, _ = ranks(ids)
    offsets = lax.dot_general(
        all_counts,
        flags((block < own_block) & (place == 0)),
        (((0,), (0,)), ((), ())),
        preferred_element_type=jnp.float32,
    )[:EXPERTS, :TOKENS]
    mix = jnp.zeros((EXPERTS * SRC_CAP, TOKENS), jnp.float32)
    for k in range(TOPK):
        turn = jnp.sum(offsets * names[k], axis=0, keepdims=True).astype(jnp.int32)
        mix = jnp.where(
            slot_iota() == packet_place(ids[k : k + 1], rank[k], turn), weights_ref[k : k + 1], mix
        )
    for part in range(3):
        rounded = mix.astype(jnp.bfloat16)
        for e in range(EXPERTS):
            for group in range(2):
                first = (e * 2 + group) * SRC_CAP
                mix_ref[part, first : first + SRC_CAP] = rounded[e * SRC_CAP : (e + 1) * SRC_CAP]
        mix = mix - rounded.astype(jnp.float32)


def way_back(counts, own_block, own_class, expert_ids, expert_weights):
    return pl.pallas_call(
        back_kernel,
        in_specs=[
            pl.BlockSpec(memory_space=pltpu.SMEM),
            pl.BlockSpec(memory_space=pltpu.VMEM),
            pl.BlockSpec(memory_space=pltpu.VMEM),
            pl.BlockSpec(memory_space=pltpu.VMEM),
        ],
        out_shape=[
            jax.ShapeDtypeStruct(counts.shape, jnp.bfloat16),
            jax.ShapeDtypeStruct((3, 2 * EXPERTS * SRC_CAP, TOKENS), jnp.bfloat16),
        ],
        compiler_params=pltpu.CompilerParams(vmem_limit_bytes=10 << 20),
        name="way_back",
    )(jnp.stack([own_block, own_class]), expert_ids.T, expert_weights.T, counts)


def final_kernel(summed_ref, combined_ref, mix_ref, out_ref):
    total = summed_ref[...]
    rows = combined_ref[...].reshape(BLOCKS * PER_CLASS, total.shape[1])
    for part in (2, 1, 0):
        total = total + lax.dot_general(
            mix_ref[part], rows, (((0,), (0,)), ((), ())), preferred_element_type=jnp.float32
        )
    out_ref[...] = total.astype(jnp.bfloat16)


def final_rows(summed, combined, mix):
    return pl.pallas_call(
        final_kernel,
        in_specs=[pl.BlockSpec(memory_space=pltpu.VMEM)] * 3,
        out_shape=jax.ShapeDtypeStruct(summed.shape, jnp.bfloat16),
        compiler_params=pltpu.CompilerParams(vmem_limit_bytes=10 << 20),
        name="final_rows",
    )(summed, combined, mix)


def shards(
    residual, queries, keys, values, lengths, norm_gain, expert_ids, expert_weights, w_in, w_out
):
    tokens, width = residual.shape
    block = ((lax.axis_index("x") * 2 + lax.axis_index("zh")) * 2 + lax.axis_index("zq")) * 4 + lax.axis_index("zn")
    own_class = lax.axis_index("zn")

    summed, outgoing = tokens_packed(block, lengths, expert_ids, residual, queries, keys, values)
    gained = (w_in.astype(jnp.float32) * norm_gain.astype(jnp.float32)[:, None]).astype(jnp.bfloat16)
    received = lax.all_to_all(outgoing, DP, split_axis=0, concat_axis=0, tiled=True)
    class_rows, place, counts = compacted(received, block, own_class)
    rows = lax.all_gather(class_rows, "zn", axis=0, tiled=True)
    core = lax.axis_index("core")
    send, rows, squares = sent_pieces(place, rows, gained, core)
    other = lax.ppermute(send, "core", ((0, 1), (1, 0)))
    own = kept_pieces(rows, squares, gained, core)
    counts, squares = lax.optimization_barrier((counts, squares))
    back, mix = way_back(counts, block, own_class, expert_ids, expert_weights)
    own, back, mix = lax.optimization_barrier((own, back, mix))
    pieces = lax.all_to_all(core_summed(own, other), "y", split_axis=0, concat_axis=0, tiled=True)
    gathered = lax.all_to_all(silu_copies(pieces), "y", split_axis=0, concat_axis=0, tiled=True)
    gathered = lax.all_gather(gathered, "core", axis=0, tiled=True)
    parts = output_parts(gathered, w_out, own_class)
    shares = [parts[0]]
    for k in (2, 3, 1):
        shares.append(lax.ppermute(parts[k], "zn", [(i, i ^ k) for i in range(CLASSES)]))
    class_out = sum(share.astype(jnp.float32) for share in shares).astype(jnp.bfloat16)
    returned = jnp.dot(
        back[:, :SLOT_ROWS], class_out, preferred_element_type=jnp.float32
    ).astype(jnp.bfloat16)
    combined = lax.all_to_all(
        returned.reshape(BLOCKS, PER_CLASS, width), DP, split_axis=0, concat_axis=0, tiled=True
    )
    return final_rows(summed, combined, mix)


def solution(mesh):
    fine = Mesh(mesh.devices.reshape(4, 2, 2, 4, 4, 2), (*DP, *TENSOR))
    in_specs = (
        P(DP, TENSOR),
        P(DP, TENSOR),
        P(DP, None, TENSOR),
        P(DP, None, TENSOR),
        P(DP),
        P(TENSOR),
        P(DP, None),
        P(DP, None),
        P(TENSOR, DP),
        P(DP, TENSOR),
    )
    return jax.shard_map(shards, mesh=fine, in_specs=in_specs, out_specs=P(DP, TENSOR), check_vma=False)
```

```python
import jax
import jax.numpy as jnp
from jax import lax
from jax.experimental import pallas as pl
from jax.experimental.pallas import tpu as pltpu
from jax.sharding import Mesh, PartitionSpec as P

HEADS = 48
KV = 8
HEAD = 128
D = 6144
EXPERTS = 8
TOPK = 2
CACHE = 128
SRC_CAP = 16
BLOCKS = 64
CLASSES = 4
PER_CLASS = SRC_CAP // CLASSES
CAPACITY = 384
CLASS_ROWS = CAPACITY // CLASSES + BLOCKS * 6 // (4 * CLASSES)
META = 128
ROWS = CAPACITY
SLOT_ROWS = CAPACITY // CLASSES
SQUARES = 16
UNIT = 128
LINES = ROWS // UNIT

NORM_EPSILON = 1e-05

DP = ("x", "zh", "zq", "zn")
TENSOR = ("y", "core")


TOKENS = 32
STEP = 32
GROUP = HEADS // KV


def ranks(ids):
    experts = lax.broadcasted_iota(jnp.int32, (EXPERTS, TOKENS), 0)
    names = [(ids[k : k + 1] == experts).astype(jnp.float32) for k in range(TOPK)]
    named = names[0] + names[1]
    before = lax.broadcasted_iota(jnp.int32, (TOKENS, TOKENS), 0) < lax.broadcasted_iota(
        jnp.int32, (TOKENS, TOKENS), 1
    )
    earlier = jnp.dot(named, before.astype(jnp.float32), preferred_element_type=jnp.float32)
    rank = [jnp.sum(earlier * name, axis=0, keepdims=True).astype(jnp.int32) for name in names]
    return names, rank, named


def slot_iota():
    return lax.broadcasted_iota(jnp.int32, (EXPERTS * SRC_CAP, TOKENS), 0)


def packet_place(ids, rank, turn):
    return ids * SRC_CAP + (rank + turn) % CLASSES * PER_CLASS + rank // CLASSES


def tokens_kernel(
    block_ref, lengths_ref, ids_ref, residual_ref, queries_ref, keys_ref, values_ref,
    summed_ref, out_ref, query_ref, attended_ref, all_ref,
):
    step = pl.program_id(0)

    @pl.when(step == 0)
    def _():
        query_ref[...] = jnp.zeros_like(query_ref)

    for h in range(GROUP):
        query_ref[:, h, :] = queries_ref[:, h * HEAD : (h + 1) * HEAD].astype(jnp.float32)
    position = lax.broadcasted_iota(jnp.int32, (8, CACHE), 1)
    scores = []
    for t in range(STEP):
        products = lax.dot_general(
            query_ref[t].astype(jnp.bfloat16),
            keys_ref[t],
            (((1,), (1,)), ((), ())),
            preferred_element_type=jnp.float32,
        ) * HEAD ** (-0.5)
        scores.append(jnp.where(position < lengths_ref[step * STEP + t], products, -1e30))
    scores = jnp.concatenate(scores, axis=0)
    powered = jnp.exp(scores - jnp.max(scores, axis=1, keepdims=True))
    probs = powered / jnp.sum(powered, axis=1, keepdims=True)
    for t in range(STEP):
        attended_ref[t] = jnp.dot(
            probs[t * 8 : (t + 1) * 8].astype(jnp.bfloat16), values_ref[t], preferred_element_type=jnp.float32
        )
    for h in range(GROUP):
        lanes = slice(h * HEAD, (h + 1) * HEAD)
        total = residual_ref[:, lanes].astype(jnp.float32) + attended_ref[:, h, :]
        summed_ref[:, lanes] = total
        all_ref[pl.ds(pl.multiple_of(step * STEP, STEP), STEP), lanes] = total

    @pl.when(step == TOKENS // STEP - 1)
    def _():
        ids = ids_ref[...]
        _, rank, named = ranks(ids)
        pick = jnp.zeros((EXPERTS * SRC_CAP, TOKENS), jnp.float32)
        for k in range(TOPK):
            pick = jnp.where(slot_iota() == packet_place(ids[k : k + 1], rank[k], block_ref[0]), 1.0, pick)
        packed = jnp.dot(
            pick.astype(jnp.bfloat16), all_ref[...].astype(jnp.bfloat16), preferred_element_type=jnp.float32
        )
        width = packed.shape[1]
        own_lane = lax.broadcasted_iota(jnp.int32, (EXPERTS, META), 0) == lax.broadcasted_iota(
            jnp.int32, (EXPERTS, META), 1
        )
        counts = jnp.sum(named, axis=1, keepdims=True)
        counts = jnp.sum(jnp.where(own_lane, counts, 0.0), axis=0, keepdims=True)
        meta = jnp.broadcast_to(counts, (PER_CLASS, META)).astype(jnp.bfloat16)
        for e in range(EXPERTS):
            for c in range(CLASSES):
                first = e * SRC_CAP + c * PER_CLASS
                rows = packed[first : first + PER_CLASS].astype(jnp.bfloat16)
                for group in range(2):
                    peer = (e * 2 + group) * CLASSES + c
                    out_ref[peer, :, :width] = rows
                    out_ref[peer, :, width:] = meta


def tokens_packed(block, lengths, expert_ids, residual, queries, keys, values):
    tokens, width = residual.shape
    whole = lambda *shape: pl.BlockSpec(shape, lambda i: (0,) * len(shape))
    return pl.pallas_call(
        tokens_kernel,
        grid=(TOKENS // STEP,),
        in_specs=[
            pl.BlockSpec(memory_space=pltpu.SMEM),
            pl.BlockSpec(memory_space=pltpu.SMEM),
            whole(TOPK, TOKENS),
            pl.BlockSpec((STEP, width), lambda i: (i, 0)),
            pl.BlockSpec((STEP, width), lambda i: (i, 0)),
            pl.BlockSpec((STEP, CACHE, HEAD), lambda i: (i, 0, 0)),
            pl.BlockSpec((STEP, CACHE, HEAD), lambda i: (i, 0, 0)),
        ],
        out_specs=[
            pl.BlockSpec((STEP, width), lambda i: (i, 0)),
            whole(BLOCKS, PER_CLASS, width + META),
        ],
        out_shape=[
            jax.ShapeDtypeStruct((tokens, width), jnp.float32),
            jax.ShapeDtypeStruct((BLOCKS, PER_CLASS, width + META), jnp.bfloat16),
        ],
        scratch_shapes=[
            pltpu.VMEM((STEP, 8, HEAD), jnp.float32),
            pltpu.VMEM((STEP, 8, HEAD), jnp.float32),
            pltpu.VMEM((TOKENS, width), jnp.float32),
        ],
        compiler_params=pltpu.CompilerParams(vmem_limit_bytes=10 << 20),
        name="tokens_packed",
    )(
        block.reshape(1),
        *(
            pltpu.with_memory_space_constraint(operand, pltpu.HBM)
            for operand in (lengths, expert_ids.T, residual, queries, keys, values)
        ),
    )


def diagonal():
    row = lax.broadcasted_iota(jnp.int32, (UNIT, UNIT), 0)
    return row == lax.broadcasted_iota(jnp.int32, (UNIT, UNIT), 1)


def leading_and_rest(sums):
    leading = sums.astype(jnp.bfloat16)
    return jnp.concatenate([leading, (sums - leading.astype(jnp.float32)).astype(jnp.bfloat16)], axis=0)


def write_pieces(rows, squares, w_ref, half, out_ref):
    columns = 2 * UNIT
    for k in range(2):
        source = (half * 2 + k) * columns
        parts = jnp.dot(
            rows,
            w_ref[:, pl.ds(pl.multiple_of(source, columns), columns)],
            preferred_element_type=jnp.float32,
        )
        for side in range(2):
            piece = k * 2 + side
            out_ref[piece, :ROWS] = parts[:, side * UNIT : (side + 1) * UNIT].astype(jnp.bfloat16)
            out_ref[piece, ROWS:] = squares


def sent_kernel(core_ref, place_ref, gathered_ref, w_ref, send_ref, rows_ref, squares_ref):
    wide = lax.dot_general(
        place_ref[...], gathered_ref[...], (((0,), (0,)), ((), ())), preferred_element_type=jnp.float32
    )
    rows = wide.astype(jnp.bfloat16)
    rows_ref[...] = rows
    sums = jnp.sum(wide * wide, axis=1, keepdims=True)
    lines = [
        jnp.sum(jnp.where(diagonal(), sums[g * UNIT : (g + 1) * UNIT], 0.0), axis=0, keepdims=True)
        for g in range(LINES)
    ]
    lines.append(jnp.zeros((SQUARES // 2 - LINES, UNIT), jnp.float32))
    squares = leading_and_rest(jnp.concatenate(lines, axis=0))
    squares_ref[...] = squares
    write_pieces(rows, squares, w_ref, 1 - core_ref[0], send_ref)


def kept_kernel(core_ref, rows_ref, squares_ref, w_ref, keep_ref):
    write_pieces(rows_ref[...], squares_ref[...], w_ref, core_ref[0], keep_ref)


def first_product(kernel, name, out_shape, core, *operands):
    return pl.pallas_call(
        kernel,
        in_specs=[
            pl.BlockSpec(memory_space=pltpu.SMEM),
            *[pl.BlockSpec(memory_space=pltpu.VMEM)] * len(operands),
        ],
        out_shape=out_shape,
        compiler_params=pltpu.CompilerParams(vmem_limit_bytes=10 << 20),
        name=name,
    )(core.reshape(1), *operands)


def half_of_units(w_in):
    return jax.ShapeDtypeStruct((w_in.shape[1] // (2 * UNIT), ROWS + SQUARES, UNIT), jnp.bfloat16)


def sent_pieces(place, gathered, w_in, core):
    out_shape = [
        half_of_units(w_in),
        jax.ShapeDtypeStruct((ROWS, gathered.shape[1]), jnp.bfloat16),
        jax.ShapeDtypeStruct((SQUARES, UNIT), jnp.bfloat16),
    ]
    return first_product(sent_kernel, "sent_pieces", out_shape, core, place, gathered, w_in)


def kept_pieces(rows, squares, w_in, core):
    return first_product(kept_kernel, "kept_pieces", half_of_units(w_in), core, rows, squares, w_in)


def core_kernel(own_ref, other_ref, out_ref):
    out_ref[:, :ROWS] = (
        own_ref[:, :ROWS].astype(jnp.float32) + other_ref[:, :ROWS].astype(jnp.float32)
    ).astype(jnp.bfloat16)
    both = own_ref[0, ROWS:].astype(jnp.float32) + other_ref[0, ROWS:].astype(jnp.float32)
    split = leading_and_rest(both[: SQUARES // 2] + both[SQUARES // 2 :])
    for piece in range(out_ref.shape[0]):
        out_ref[piece, ROWS:] = split


def core_summed(own, other):
    return pl.pallas_call(
        core_kernel,
        out_shape=jax.ShapeDtypeStruct(own.shape, jnp.bfloat16),
        compiler_params=pltpu.CompilerParams(vmem_limit_bytes=10 << 20),
        name="core_summed",
    )(own, other)


def silu_kernel(in_ref, out_ref):
    total = in_ref[0].astype(jnp.float32)
    for piece in range(1, in_ref.shape[0]):
        total = total + in_ref[piece].astype(jnp.float32)
    squares = total[ROWS : ROWS + SQUARES // 2] + total[ROWS + SQUARES // 2 :]
    for g in range(LINES):
        own = jnp.sum(jnp.where(diagonal(), squares[g : g + 1], 0.0), axis=1, keepdims=True)
        scaled = total[g * UNIT : (g + 1) * UNIT] * lax.rsqrt(own / D + NORM_EPSILON)
        hidden = (scaled / (1.0 + jnp.exp(-scaled))).astype(jnp.bfloat16)
        for piece in range(out_ref.shape[0]):
            out_ref[piece, g * UNIT : (g + 1) * UNIT] = hidden


def silu_copies(pieces):
    return pl.pallas_call(
        silu_kernel,
        out_shape=jax.ShapeDtypeStruct((pieces.shape[0], ROWS, UNIT), jnp.bfloat16),
        compiler_params=pltpu.CompilerParams(vmem_limit_bytes=10 << 20),
        name="silu_copies",
    )(pieces)


def output_kernel(class_ref, hidden_ref, w_ref, *refs):
    *out_refs, whole_ref = refs
    hidden = jnp.concatenate([hidden_ref[piece] for piece in range(hidden_ref.shape[0])], axis=1)
    whole_ref[...] = jnp.dot(hidden, w_ref[...], preferred_element_type=jnp.float32).astype(jnp.bfloat16)
    for k, out_ref in enumerate(out_refs):
        start = pl.multiple_of((class_ref[0] ^ k) * SLOT_ROWS, SLOT_ROWS)
        out_ref[...] = whole_ref[pl.ds(start, SLOT_ROWS)]


def output_parts(hidden, w_out, own_class):
    part = jax.ShapeDtypeStruct((SLOT_ROWS, w_out.shape[1]), jnp.bfloat16)
    return pl.pallas_call(
        output_kernel,
        in_specs=[
            pl.BlockSpec(memory_space=pltpu.SMEM),
            pl.BlockSpec(memory_space=pltpu.VMEM),
            pl.BlockSpec(memory_space=pltpu.VMEM),
        ],
        out_shape=[part] * CLASSES,
        scratch_shapes=[pltpu.VMEM((ROWS, w_out.shape[1]), jnp.bfloat16)],
        compiler_params=pltpu.CompilerParams(vmem_limit_bytes=10 << 20),
        name="output_parts",
    )(own_class.reshape(1), hidden, w_out)


def flags(condition):
    return condition.astype(jnp.float32).astype(jnp.bfloat16)


def kept_of_blocks(all_counts, own_block):
    slots = all_counts.shape[0]
    row = lax.broadcasted_iota(jnp.int32, (slots, slots), 0)
    column = lax.broadcasted_iota(jnp.int32, (slots, slots), 1)
    earlier = flags(((column & 3) == 0) & (column < (row & -4)))

    def earlier_sum(counts):
        return jnp.dot(earlier, counts, preferred_element_type=jnp.float32).astype(jnp.int32)

    own_expert = own_block >> 3
    counts = jnp.dot(
        all_counts,
        flags(lax.broadcasted_iota(jnp.int32, (META, META), 0) == own_expert),
        preferred_element_type=jnp.float32,
    )
    offset = earlier_sum(counts.astype(jnp.bfloat16))
    return offset, jnp.clip(CAPACITY - offset, 0, counts.astype(jnp.int32)), earlier_sum


def compact_kernel(here_ref, received_ref, rows_ref, place_ref, counts_ref):
    width = rows_ref.shape[1]
    own_class = here_ref[1]
    received = received_ref[...].reshape(BLOCKS * PER_CLASS, width + META)
    all_counts = received[:, width:]
    counts_ref[...] = all_counts
    offset, kept, earlier_sum = kept_of_blocks(all_counts, here_ref[0])
    line = lax.broadcasted_iota(jnp.int32, kept.shape, 0)
    lane = lax.broadcasted_iota(jnp.int32, kept.shape, 1)
    block, place = line >> 2, line & 3

    shift = (own_class + (lane >> 5) + BLOCKS - block) & 3
    in_class = (kept - shift + 3) >> 2
    first = earlier_sum(in_class.astype(jnp.float32).astype(jnp.bfloat16))
    live = place < in_class
    spot = jnp.where(live, first + place, -1)
    slot = jnp.where(live, offset + place * 4 + shift + 1, 0)
    digits = jnp.where((lane & 16) == 0, slot >> 4, slot & 15).astype(jnp.float32).astype(jnp.bfloat16)

    for turn in range(CLASSES):
        start = turn * 32
        chosen = flags(spot[:, start : start + 1] == lane)
        if turn == 0:
            rows = lax.dot_general(
                chosen, received[:, :width], (((0,), (0,)), ((), ())), preferred_element_type=jnp.float32
            )
            rows_ref[...] = rows[:CLASS_ROWS].astype(jnp.bfloat16)
        found = lax.dot_general(chosen, digits, (((0,), (0,)), ((), ())), preferred_element_type=jnp.float32)
        found = found[:CLASS_ROWS, start : start + 1] * 16.0 + found[:CLASS_ROWS, start + 16 : start + 17]
        found = found.astype(jnp.int32) - 1
        target = jnp.where(found < 0, -1, (found & 3) * SLOT_ROWS + (found >> 2))
        of_class = (own_class + turn) & 3
        place_ref[pl.ds(pl.multiple_of(of_class * CLASS_ROWS, 8), CLASS_ROWS)] = flags(
            target == lax.broadcasted_iota(jnp.int32, (CLASS_ROWS, ROWS), 1)
        )


def compacted(received, own_block, own_class):
    blocks, places, wide = received.shape
    return pl.pallas_call(
        compact_kernel,
        in_specs=[
            pl.BlockSpec(memory_space=pltpu.SMEM),
            pl.BlockSpec(memory_space=pltpu.VMEM),
        ],
        out_shape=[
            jax.ShapeDtypeStruct((CLASS_ROWS, wide - META), jnp.bfloat16),
            jax.ShapeDtypeStruct((CLASSES * CLASS_ROWS, ROWS), jnp.bfloat16),
            jax.ShapeDtypeStruct((blocks * places, META), jnp.bfloat16),
        ],
        compiler_params=pltpu.CompilerParams(vmem_limit_bytes=10 << 20),
        name="compacted",
    )(jnp.stack([own_block, own_class]), received)


def back_kernel(here_ref, ids_ref, weights_ref, counts_ref, back_ref, mix_ref):
    own_block, own_class = here_ref[0], here_ref[1]
    all_counts = counts_ref[...]
    offset, kept, _ = kept_of_blocks(all_counts, own_block)
    line = lax.broadcasted_iota(jnp.int32, kept.shape, 0)
    lane = lax.broadcasted_iota(jnp.int32, kept.shape, 1)
    block, place = line >> 2, line & 3
    rank = place * 4 + ((own_class - offset) & 3)
    back_ref[...] = flags(((offset + rank - own_class) >> 2 == lane) & (rank < kept))

    ids = ids_ref[...]
    names, rank, _ = ranks(ids)
    offsets = lax.dot_general(
        all_counts,
        flags((block < own_block) & (place == 0)),
        (((0,), (0,)), ((), ())),
        preferred_element_type=jnp.float32,
    )[:EXPERTS, :TOKENS]
    mix = jnp.zeros((EXPERTS * SRC_CAP, TOKENS), jnp.float32)
    for k in range(TOPK):
        turn = jnp.sum(offsets * names[k], axis=0, keepdims=True).astype(jnp.int32)
        mix = jnp.where(
            slot_iota() == packet_place(ids[k : k + 1], rank[k], turn), weights_ref[k : k + 1], mix
        )
    for part in range(3):
        rounded = mix.astype(jnp.bfloat16)
        for e in range(EXPERTS):
            for group in range(2):
                first = (e * 2 + group) * SRC_CAP
                mix_ref[part, first : first + SRC_CAP] = rounded[e * SRC_CAP : (e + 1) * SRC_CAP]
        mix = mix - rounded.astype(jnp.float32)


def way_back(counts, own_block, own_class, expert_ids, expert_weights):
    return pl.pallas_call(
        back_kernel,
        in_specs=[
            pl.BlockSpec(memory_space=pltpu.SMEM),
            pl.BlockSpec(memory_space=pltpu.VMEM),
            pl.BlockSpec(memory_space=pltpu.VMEM),
            pl.BlockSpec(memory_space=pltpu.VMEM),
        ],
        out_shape=[
            jax.ShapeDtypeStruct(counts.shape, jnp.bfloat16),
            jax.ShapeDtypeStruct((3, 2 * EXPERTS * SRC_CAP, TOKENS), jnp.bfloat16),
        ],
        compiler_params=pltpu.CompilerParams(vmem_limit_bytes=10 << 20),
        name="way_back",
    )(jnp.stack([own_block, own_class]), expert_ids.T, expert_weights.T, counts)


def final_kernel(summed_ref, combined_ref, mix_ref, out_ref):
    total = summed_ref[...]
    rows = combined_ref[...].reshape(BLOCKS * PER_CLASS, total.shape[1])
    for part in (2, 1, 0):
        total = total + lax.dot_general(
            mix_ref[part], rows, (((0,), (0,)), ((), ())), preferred_element_type=jnp.float32
        )
    out_ref[...] = total.astype(jnp.bfloat16)


def final_rows(summed, combined, mix):
    return pl.pallas_call(
        final_kernel,
        in_specs=[pl.BlockSpec(memory_space=pltpu.VMEM)] * 3,
        out_shape=jax.ShapeDtypeStruct(summed.shape, jnp.bfloat16),
        compiler_params=pltpu.CompilerParams(vmem_limit_bytes=10 << 20),
        name="final_rows",
    )(summed, combined, mix)


def shards(
    residual, queries, keys, values, lengths, norm_gain, expert_ids, expert_weights, w_in, w_out
):
    tokens, width = residual.shape
    block = ((lax.axis_index("x") * 2 + lax.axis_index("zh")) * 2 + lax.axis_index("zq")) * 4 + lax.axis_index("zn")
    own_class = lax.axis_index("zn")

    summed, outgoing = tokens_packed(block, lengths, expert_ids, residual, queries, keys, values)
    gained = (w_in.astype(jnp.float32) * norm_gain.astype(jnp.float32)[:, None]).astype(jnp.bfloat16)
    received = lax.all_to_all(outgoing, DP, split_axis=0, concat_axis=0, tiled=True)
    class_rows, place, counts = compacted(received, block, own_class)
    rows = lax.all_gather(class_rows, "zn", axis=0, tiled=True)
    core = lax.axis_index("core")
    send, rows, squares = sent_pieces(place, rows, gained, core)
    other = lax.ppermute(send, "core", ((0, 1), (1, 0)))
    own = kept_pieces(rows, squares, gained, core)
    counts, squares = lax.optimization_barrier((counts, squares))
    back, mix = way_back(counts, block, own_class, expert_ids, expert_weights)
    own, back, mix = lax.optimization_barrier((own, back, mix))
    pieces = lax.all_to_all(core_summed(own, other), "y", split_axis=0, concat_axis=0, tiled=True)
    gathered = lax.all_to_all(silu_copies(pieces), "y", split_axis=0, concat_axis=0, tiled=True)
    gathered = lax.all_gather(gathered, "core", axis=0, tiled=True)
    parts = output_parts(gathered, w_out, own_class)
    shares = [parts[0]]
    for k in (2, 3, 1):
        shares.append(lax.ppermute(parts[k], "zn", [(i, i ^ k) for i in range(CLASSES)]))
    class_out = sum(share.astype(jnp.float32) for share in shares).astype(jnp.bfloat16)
    returned = jnp.dot(
        back[:, :SLOT_ROWS], class_out, preferred_element_type=jnp.float32
    ).astype(jnp.bfloat16)
    combined = lax.all_to_all(
        returned.reshape(BLOCKS, PER_CLASS, width), DP, split_axis=0, concat_axis=0, tiled=True
    )
    return final_rows(summed, combined, mix)


def solution(mesh):
    fine = Mesh(mesh.devices.reshape(4, 2, 2, 4, 4, 2), (*DP, *TENSOR))
    in_specs = (
        P(DP, TENSOR),
        P(DP, TENSOR),
        P(DP, None, TENSOR),
        P(DP, None, TENSOR),
        P(DP),
        P(TENSOR),
        P(DP, None),
        P(DP, None),
        P(TENSOR, DP),
        P(DP, TENSOR),
    )
    return jax.shard_map(shards, mesh=fine, in_specs=in_specs, out_specs=P(DP, TENSOR), check_vma=False)
```
